32 devices in a mesh: fsdp: 4 (over y, x), seq: 8 (over z, core).
Axes of the slice: x: 2, y: 2, z: 4, core: 2. Of those that a mesh axis runs over, the one named last changes fastest.
Arguments:
- layer_input: bfloat16 [4, 1024, 1024], P('fsdp', 'seq'), may hold values from -6 to 6
- first_layer_values: bfloat16 [4, 1024, 1024], P('fsdp', 'seq'), may hold values from -6 to 6
- document_numbers: int32 [4, 1024], P('fsdp', 'seq'), may hold values from 0 to 1, as said below
- output_cotangent: bfloat16 [4, 1024, 1024], P('fsdp', 'seq'), may hold values from -6 to 6
- projection_matrices: bfloat16 [3, 1024, 1024], P(None, None, 'fsdp'), may hold values from -0.1875 to 0.1875
- time_output_matrix: bfloat16 [1024, 1024], P('fsdp'), may hold values from -0.25 to 0.25
- lowrank_first: bfloat16 [1024, 288], P('fsdp'), may hold values from -0.1875 to 0.1875
- lowrank_second: bfloat16 [288, 1024], P(None, 'fsdp'), may hold values from -0.75 to 0.75
- channel_key_matrix: bfloat16 [1024, 4096], P(None, 'fsdp'), may hold values from -0.1875 to 0.1875
- channel_value_matrix: bfloat16 [4096, 1024], P('fsdp'), may hold values from -0.09375 to 0.09375
- vectors: bfloat16 [19, 1024], P(None, 'fsdp'), may hold values from -8 to 2, as said below
Outputs:
- block_out: bfloat16 [4, 1024, 1024], P('fsdp', 'seq')
- d_input: float32 [4, 1024, 1024], P('fsdp', 'seq')
- d_v_first: float32 [4, 1024, 1024], P('fsdp', 'seq')
- grad_proj: float32 [3, 1024, 1024], P(None, None, 'fsdp')
- grad_out_weight: float32 [1024, 1024], P('fsdp')
- grad_lora_down: float32 [1024, 288], P('fsdp')
- grad_lora_up: float32 [288, 1024], P(None, 'fsdp')
- grad_key_weight: float32 [1024, 4096], P(None, 'fsdp')
- grad_value_weight: float32 [4096, 1024], P('fsdp')
- grad_vectors: float32 [19, 1024], P(None, 'fsdp')
The draws below stay inside these ranges and needn't reach their ends.
Inputs may be any that keep to these rules, and one draw needn't show every extreme that they name: `document_numbers`: in each sequence the ids start at 0, never fall, rise by one at each new document and end at 1; every document holds 128 tokens or more. `vectors`: rows 0 to 5 and 18 lie in 0 to 1, row 6 in -8 to -1, rows 7 and 8 in -2 to 2, rows 9, 10, 12, 14, 16 in 0.5 to 1.5, row 11 in -0.25 to 0.25, rows 13, 15, 17 in -0.5 to 0.5.
All inputs are finite; a program needn't handle non-finite values.
Results may differ from the reference program's by a relative error of at most 0.024.
Values may be sent and summed in bfloat16 or wider, within the bound.
No kernel may reach another device: no remote copies, remote signals or barrier semaphores. Data moves between devices by JAX's collectives and lax.ppermute only.
A program may use at most 256 MiB of HBM per device.

```python
import jax
import jax.numpy as jnp
from jax import lax

MODEL_WIDTH = 1024
ATTENTION_GROUPS = 16
ATTN_SLICE_SIZE = 64
FF = 4096
DECAY_INNER = 64
RATE_INNER = 64
VALUE_MIX_INNER = 32
INNER_TOTAL = 288
NVEC = 19
LEN = 1024
SEQS = 4
NDOC = 2


def draw_document_numbers(key, part):

    def one_sequence(seq_key):
        grid_key, offset_key = jax.random.split(seq_key)
        cells = 2 * NDOC
        unit_len = LEN // cells
        order = jax.random.permutation(grid_key, cells - 1)
        chosen = order[:NDOC - 1] + 1
        offsets = jax.random.randint(offset_key, (NDOC - 1,), 0, max(unit_len // 2, 1))
        cut_points = chosen * unit_len + offsets
        marks = jnp.zeros((LEN,), jnp.int32).at[cut_points].add(1)
        return jnp.cumsum(marks).astype(jnp.int32)
    seq_keys = jax.random.split(key, SEQS)
    return jax.vmap(one_sequence)(seq_keys)


def draw_vectors(key, part):
    lows = jnp.array([0.0, 0.0, 0.0, 0.0, 0.0, 0.0, -8.0, -2.0, -2.0, 0.5, 0.5, -0.25, 0.5, -0.5, 0.5, -0.5, 0.5, -0.5, 0.0], jnp.float32)
    highs = jnp.array([1.0, 1.0, 1.0, 1.0, 1.0, 1.0, -1.0, 2.0, 2.0, 1.5, 1.5, 0.25, 1.5, 0.5, 1.5, 0.5, 1.5, 0.5, 1.0], jnp.float32)
    spots = jax.random.uniform(key, (NVEC, MODEL_WIDTH), jnp.float32)
    return (lows[:, None] + (highs - lows)[:, None] * spots).astype(jnp.bfloat16)


def level_of(key, shape, cuts, smallest, largest):
    def one(position, blocks):
        draws = jax.random.uniform(jax.random.fold_in(jax.random.fold_in(key, 6), position), (blocks,), jnp.float32, smallest / len(cuts), largest / len(cuts))
        return jnp.repeat(jnp.exp(draws), shape[position] // blocks).reshape((-1,) + (1,) * (len(shape) - position - 1))

    loudness = one(*cuts[0])
    for cut in cuts[1:]:
        loudness = loudness * one(*cut)
    return loudness


def noise(key, dims, width, most, cuts=(), dtype=jnp.bfloat16):
    level = level_of(key, dims, cuts, -0.22, 0.18) if cuts else 1.0
    values = jax.random.normal(key, dims, jnp.float32) * width * level
    return jnp.minimum(jnp.maximum(values, -most), most).astype(dtype)


def setup_inputs(seed: int = 0) -> dict:
    arg_keys = jax.random.split(jax.random.key(seed), 12)
    return {
        "layer_input": noise(arg_keys[0], (SEQS, LEN, MODEL_WIDTH), 1.0, 6.0, ((0, 4), (1, 8))),
        "first_layer_values": noise(arg_keys[1], (SEQS, LEN, MODEL_WIDTH), 1.0, 6.0, ((0, 4), (1, 8))),
        "document_numbers": draw_document_numbers(jax.random.fold_in(arg_keys[11], 71), 0),
        "output_cotangent": noise(arg_keys[3], (SEQS, LEN, MODEL_WIDTH), 1.0, 6.0, ((0, 4), (1, 8))),
        "projection_matrices": noise(arg_keys[4], (3, MODEL_WIDTH, MODEL_WIDTH), MODEL_WIDTH ** -0.5, 0.1875, ((2, 4),)),
        "time_output_matrix": noise(arg_keys[5], (MODEL_WIDTH, MODEL_WIDTH), (MODEL_WIDTH // 2) ** -0.5, 0.25, ((0, 4),)),
        "lowrank_first": noise(arg_keys[6], (MODEL_WIDTH, INNER_TOTAL), MODEL_WIDTH ** -0.5, 0.1875, ((0, 4),)),
        "lowrank_second": noise(arg_keys[7], (INNER_TOTAL, MODEL_WIDTH), DECAY_INNER ** -0.5, 0.75, ((1, 4),)),
        "channel_key_matrix": noise(arg_keys[8], (MODEL_WIDTH, FF), MODEL_WIDTH ** -0.5, 0.1875, ((1, 4),)),
        "channel_value_matrix": noise(arg_keys[9], (FF, MODEL_WIDTH), FF ** -0.5, 0.09375, ((0, 4),)),
        "vectors": draw_vectors(jax.random.fold_in(arg_keys[11], 71), 0),
    }


LN_EPS = 1e-05
GROUP_EPS = 0.00064
UNIT_EPS = 1e-06

def matmul(left, right):
    return jnp.dot(left, right, preferred_element_type=jnp.float32)

def layer_norm(values, gain, bias_row):
    center = values - lax.optimization_barrier(jnp.mean(values, axis=-1, keepdims=True))
    spread = lax.optimization_barrier(jnp.mean(center * center, axis=-1, keepdims=True))
    return center * lax.rsqrt(spread + LN_EPS) * gain + bias_row

def blend_rows(current, earlier, keep_row, gain_rows):
    change = earlier * keep_row - current
    return current[None] + change[None] * gain_rows[:, None, :]

def shift_down(source):
    return jnp.concatenate([jnp.zeros_like(source[:1]), source[:-1]])

def shift_up(source):
    return jnp.concatenate([source[1:], jnp.zeros_like(source[:1])])

def prepare(key_raw, value_raw, decay_up, alpha_up, vmix_up, first_value, arrays_single_precision):
    sequence_item_array = key_raw.shape[0]
    w_log = -jax.nn.softplus(-(arrays_single_precision[6] + decay_up)) - 0.5
    log_decay = -jnp.exp(w_log)
    alpha_gate = jax.nn.sigmoid(arrays_single_precision[7] + alpha_up)
    value_gate = jax.nn.sigmoid(arrays_single_precision[8] + vmix_up)
    merged_payload_vector = value_raw + (first_value - value_raw) * value_gate
    unit_key = (key_raw * arrays_single_precision[9]).reshape(sequence_item_array, ATTENTION_GROUPS, ATTN_SLICE_SIZE)
    unit_key = unit_key * lax.rsqrt(lax.optimization_barrier(jnp.sum(unit_key * unit_key, axis=-1, keepdims=True)) + UNIT_EPS)
    unit_key = unit_key.reshape(sequence_item_array, ATTENTION_GROUPS * ATTN_SLICE_SIZE)
    lookup_scaled_entry = key_raw * (1.0 + (alpha_gate - 1.0) * arrays_single_precision[10])
    return (log_decay, lookup_scaled_entry, merged_payload_vector, -unit_key, unit_key * alpha_gate)

def finish(outputs, acceptor_entries, lookup_scaled_entry, merged_payload_vector, sigmoid_upper_factor, arrays_single_precision):
    sequence_item_array = outputs.shape[0]
    grouped = outputs.reshape(sequence_item_array, ATTENTION_GROUPS, ATTN_SLICE_SIZE)
    center = grouped - lax.optimization_barrier(jnp.mean(grouped, axis=-1, keepdims=True))
    spread = lax.optimization_barrier(jnp.mean(center * center, axis=-1, keepdims=True))
    standardized_entering = (center * lax.rsqrt(spread + GROUP_EPS)).reshape(sequence_item_array, ATTENTION_GROUPS * ATTN_SLICE_SIZE) * arrays_single_precision[12] + arrays_single_precision[13]
    extra_current_array = lax.optimization_barrier(jnp.sum((acceptor_entries * lookup_scaled_entry * arrays_single_precision[11]).reshape(sequence_item_array, ATTENTION_GROUPS, ATTN_SLICE_SIZE), axis=-1, keepdims=True))
    extra_current_term = (extra_current_array * merged_payload_vector.reshape(sequence_item_array, ATTENTION_GROUPS, ATTN_SLICE_SIZE)).reshape(sequence_item_array, ATTENTION_GROUPS * ATTN_SLICE_SIZE)
    return (standardized_entering + extra_current_term) * sigmoid_upper_factor

def recurrence(acceptor_entries, log_decay, lookup_scaled_entry, merged_payload_vector, a_vec, b_vec, start_flag):
    sequence_item_array = acceptor_entries.shape[0]

    def by_heads(source):
        return source.reshape(sequence_item_array, ATTENTION_GROUPS, ATTN_SLICE_SIZE)

    def advance(carried, token_step):
        r_tok, d_tok, k_tok, v_tok, a_tok, b_tok, s_tok = token_step
        carried = carried * (1.0 - s_tok)
        pulled = lax.optimization_barrier(jnp.sum(carried * a_tok[:, None, :], axis=-1))
        carried = carried * jnp.exp(d_tok)[:, None, :] + pulled[:, :, None] * b_tok[:, None, :] + v_tok[:, :, None] * k_tok[:, None, :]
        return (carried, lax.optimization_barrier(jnp.sum(carried * r_tok[:, None, :], axis=-1)))
    initial = jnp.zeros((ATTENTION_GROUPS, ATTN_SLICE_SIZE, ATTN_SLICE_SIZE), jnp.float32)
    sources = (by_heads(acceptor_entries), by_heads(log_decay), by_heads(lookup_scaled_entry), by_heads(merged_payload_vector), by_heads(a_vec), by_heads(b_vec), start_flag)
    _, outputs = lax.scan(jax.checkpoint(advance), initial, sources)
    return outputs.reshape(sequence_item_array, ATTENTION_GROUPS * ATTN_SLICE_SIZE)

def reference(layer_input, first_layer_values, document_numbers, output_cotangent, projection_matrices, time_output_matrix, lowrank_first, lowrank_second, channel_key_matrix, channel_value_matrix, vectors):
    arrays_single_precision = vectors.astype(jnp.float32)
    lowrank_bounds = (0, DECAY_INNER, DECAY_INNER + RATE_INNER, DECAY_INNER + RATE_INNER + VALUE_MIX_INNER, INNER_TOTAL)
    down_shards = [lowrank_first[:, lowrank_bounds[belongs_flag]:lowrank_bounds[belongs_flag + 1]] for belongs_flag in range(4)]
    second_shards = [lowrank_second[lowrank_bounds[belongs_flag]:lowrank_bounds[belongs_flag + 1]] for belongs_flag in range(4)]

    def sequence_step(totals, inputs_seq):
        tokens, first_seq, ids_seq, cotangent = inputs_seq
        resid_in = tokens.astype(jnp.float32)
        earlier_ids = jnp.concatenate([jnp.full((1,), -1, jnp.int32), ids_seq[:-1]])
        start_flag = (ids_seq != earlier_ids).astype(jnp.float32)
        keep_row = (1.0 - start_flag)[:, None]

        def mixer(current, earlier, gain_rows):
            return blend_rows(current, earlier, keep_row, gain_rows)
        normed_one, ln_one_back = jax.vjp(layer_norm, resid_in, arrays_single_precision[14], arrays_single_precision[15])
        mixed_rows, mix_back = jax.vjp(mixer, normed_one, shift_down(normed_one), arrays_single_precision[0:6])
        mixed_b = mixed_rows.astype(jnp.bfloat16)
        acceptor_entries = matmul(mixed_b[0], projection_matrices[0])
        key_raw = matmul(mixed_b[2], projection_matrices[1])
        value_raw = matmul(mixed_b[3], projection_matrices[2])
        decay_pre = matmul(mixed_b[1], down_shards[0])
        low_decay = jnp.tanh(decay_pre).astype(jnp.bfloat16)
        low_alpha = matmul(mixed_b[4], down_shards[1]).astype(jnp.bfloat16)
        low_vmix = matmul(mixed_b[3], down_shards[2]).astype(jnp.bfloat16)
        gate_pre = matmul(mixed_b[5], down_shards[3])
        low_gate = jax.nn.sigmoid(gate_pre).astype(jnp.bfloat16)
        decay_up = matmul(low_decay, second_shards[0])
        alpha_up = matmul(low_alpha, second_shards[1])
        vmix_up = matmul(low_vmix, second_shards[2])
        sigmoid_upper_factor = matmul(low_gate, second_shards[3])
        prepared, prep_back = jax.vjp(prepare, key_raw, value_raw, decay_up, alpha_up, vmix_up, first_seq.astype(jnp.float32), arrays_single_precision)
        log_decay, lookup_scaled_entry, merged_payload_vector, a_vec, b_vec = prepared

        def runner(recept_in, decay_in, key_in, value_in, avec_in, bvec_in):
            return recurrence(recept_in, decay_in, key_in, value_in, avec_in, bvec_in, start_flag)
        outputs, wkv_back = jax.vjp(runner, acceptor_entries, log_decay, lookup_scaled_entry, merged_payload_vector, a_vec, b_vec)
        branch, fin_back = jax.vjp(finish, outputs, acceptor_entries, lookup_scaled_entry, merged_payload_vector, sigmoid_upper_factor, arrays_single_precision)
        branch_b = branch.astype(jnp.bfloat16)
        middle = resid_in + matmul(branch_b, time_output_matrix)
        normed_two, ln_two_back = jax.vjp(layer_norm, middle, arrays_single_precision[16], arrays_single_precision[17])
        cmix_in, cmix_back = jax.vjp(mixer, normed_two, shift_down(normed_two), arrays_single_precision[18:19])
        cmix_b = cmix_in[0].astype(jnp.bfloat16)
        pre_act = matmul(cmix_b, channel_key_matrix)
        hidden_b = jnp.square(jax.nn.relu(pre_act)).astype(jnp.bfloat16)
        block_out = (middle + matmul(hidden_b, channel_value_matrix)).astype(jnp.bfloat16)
        grad_value = matmul(hidden_b.T, cotangent)
        d_pre_b = (matmul(cotangent, channel_value_matrix.T) * 2.0 * jax.nn.relu(pre_act)).astype(jnp.bfloat16)
        grad_key = matmul(cmix_b.T, d_pre_b)
        d_cmix = matmul(d_pre_b, channel_key_matrix.T)
        d_normed_two, d_earlier_two, d_cmix_gain = cmix_back(d_cmix[None])
        d_middle, d_gain_two, d_bias_two = ln_two_back(d_normed_two + shift_up(d_earlier_two))
        d_middle = d_middle + cotangent.astype(jnp.float32)
        d_middle_b = d_middle.astype(jnp.bfloat16)
        grad_out = matmul(branch_b.T, d_middle_b)
        d_branch = matmul(d_middle_b, time_output_matrix.T)
        d_outputs, d_recept_a, d_key_a, d_value_a, d_gate_up, d_vec_fin = fin_back(d_branch)
        d_recept_b, d_decay, d_key_b, d_value_b, d_avec, d_bvec = wkv_back(d_outputs)
        prep_grads = prep_back((d_decay, d_key_a + d_key_b, d_value_a + d_value_b, d_avec, d_bvec))
        d_key_raw, d_value_raw, d_decay_up, d_alpha_up, d_vmix_up, d_first, d_vec_prep = prep_grads
        recept_g = (d_recept_a + d_recept_b).astype(jnp.bfloat16)
        key_g = d_key_raw.astype(jnp.bfloat16)
        value_g = d_value_raw.astype(jnp.bfloat16)
        decay_g = d_decay_up.astype(jnp.bfloat16)
        alpha_g = d_alpha_up.astype(jnp.bfloat16)
        vmix_g = d_vmix_up.astype(jnp.bfloat16)
        gate_g = d_gate_up.astype(jnp.bfloat16)
        grad_up = jnp.concatenate([matmul(low_decay.T, decay_g), matmul(low_alpha.T, alpha_g), matmul(low_vmix.T, vmix_g), matmul(low_gate.T, gate_g)], axis=0)
        tanh_now = jnp.tanh(decay_pre)
        low_decay_g = (matmul(decay_g, second_shards[0].T) * (1.0 - tanh_now * tanh_now)).astype(jnp.bfloat16)
        low_alpha_g = matmul(alpha_g, second_shards[1].T).astype(jnp.bfloat16)
        low_vmix_g = matmul(vmix_g, second_shards[2].T).astype(jnp.bfloat16)
        sigma_now = jax.nn.sigmoid(gate_pre)
        low_gate_g = (matmul(gate_g, second_shards[3].T) * sigma_now * (1.0 - sigma_now)).astype(jnp.bfloat16)
        grad_down = jnp.concatenate([matmul(mixed_b[1].T, low_decay_g), matmul(mixed_b[4].T, low_alpha_g), matmul(mixed_b[3].T, low_vmix_g), matmul(mixed_b[5].T, low_gate_g)], axis=1)
        grad_proj = jnp.stack([matmul(mixed_b[0].T, recept_g), matmul(mixed_b[2].T, key_g), matmul(mixed_b[3].T, value_g)])
        d_mixed = jnp.stack([matmul(recept_g, projection_matrices[0].T), matmul(low_decay_g, down_shards[0].T), matmul(key_g, projection_matrices[1].T), matmul(value_g, projection_matrices[2].T) + matmul(low_vmix_g, down_shards[2].T), matmul(low_alpha_g, down_shards[1].T), matmul(low_gate_g, down_shards[3].T)])
        d_normed_one, d_earlier_one, d_mix_gains = mix_back(d_mixed)
        d_resid, d_gain_one, d_bias_one = ln_one_back(d_normed_one + shift_up(d_earlier_one))
        d_input = d_resid + d_middle
        grad_vec = d_vec_fin + d_vec_prep
        grad_vec = grad_vec.at[0:6].add(d_mix_gains).at[14].add(d_gain_one).at[15].add(d_bias_one)
        grad_vec = grad_vec.at[16].add(d_gain_two).at[17].add(d_bias_two).at[18].add(d_cmix_gain[0])
        gradients = (grad_proj, grad_out, grad_down, grad_up, grad_key, grad_value, grad_vec)
        totals = jax.tree.map(jnp.add, totals, gradients)
        return (totals, (block_out, d_input, d_first))
    initial_zeroes = (jnp.zeros(projection_matrices.shape, jnp.float32), jnp.zeros(time_output_matrix.shape, jnp.float32), jnp.zeros(lowrank_first.shape, jnp.float32), jnp.zeros(lowrank_second.shape, jnp.float32), jnp.zeros(channel_key_matrix.shape, jnp.float32), jnp.zeros(channel_value_matrix.shape, jnp.float32), jnp.zeros(vectors.shape, jnp.float32))
    totals, stacked = lax.scan(sequence_step, initial_zeroes, (layer_input, first_layer_values, document_numbers, output_cotangent))
    return (stacked[0], stacked[1], stacked[2], totals[0], totals[1], totals[2], totals[3], totals[4], totals[5], totals[6])
```

```python
import jax
import jax.numpy as jnp
from jax import lax
from jax.experimental import pallas as pl
from jax.experimental.pallas import tpu as pltpu
from jax.sharding import PartitionSpec as P

F32 = jnp.float32
BF16 = jnp.bfloat16
HEAD = 64
PAIR = 128
BOUNDS = (0, 64, 128, 160, 288)
LN_EPS = 1e-05
GROUP_EPS = 0.00064
UNIT_EPS = 1e-06
NN = (((1,), (0,)), ((), ()))
NT = (((1,), (1,)), ((), ()))
TN = (((0,), (0,)), ((), ()))


def mm(left, right, dims=NN):
    return lax.dot_general(
        left.astype(BF16), right.astype(BF16), dims, preferred_element_type=F32
    )


def mm_exact_left(left, right, dims=NN):
    high = right.astype(BF16)
    low = (right - high.astype(F32)).astype(BF16)
    return lax.dot_general(left, high, dims, preferred_element_type=F32) + lax.dot_general(
        left, low, dims, preferred_element_type=F32
    )


def mm_exact_right(left, right):
    high = left.astype(BF16)
    low = (left - high.astype(F32)).astype(BF16)
    return lax.dot_general(high, right, NN, preferred_element_type=F32) + lax.dot_general(
        low, right, NN, preferred_element_type=F32
    )


def lane_halves(shape):
    lane = lax.broadcasted_iota(jnp.int32, shape, 1)
    return lane < HEAD


def halves(array):
    first = lane_halves(array.shape)
    zero = jnp.zeros_like(array)
    return (jnp.where(first, array, zero), jnp.where(first, zero, array))


def head_sums(array):
    row = lax.broadcasted_iota(jnp.int32, (PAIR, PAIR), 0)
    col = lax.broadcasted_iota(jnp.int32, (PAIR, PAIR), 1)
    ones = jnp.where((row < HEAD) == (col < HEAD), 1.0, 0.0).astype(BF16)
    return mm_exact_right(array, ones)


def compact(block):
    return jnp.where(lane_halves((HEAD, PAIR)), block[:HEAD], block[HEAD:])


def spread(pair):
    return jnp.concatenate(halves(pair), axis=0)


def prepared(kr, vr, du, au, vu, fv, vec):
    decay_in = vec[6:7] + du
    sig = jax.nn.sigmoid(decay_in)
    ld = sig * (-0.6065306597126334)
    alpha = jax.nn.sigmoid(vec[7:8] + au)
    vg = jax.nn.sigmoid(vec[8:9] + vu)
    mv = vr + (fv - vr) * vg
    raw_unit = kr * vec[9:10]
    scale = lax.rsqrt(head_sums(raw_unit * raw_unit) + UNIT_EPS)
    unit = raw_unit * scale
    mult = 1.0 + (alpha - 1.0) * vec[10:11]
    sk = kr * mult
    return (sig, ld, alpha, vg, mv, scale, unit, mult, sk)


def scaled_parts(r, ld, sk, unit, alpha, seg_col, seg_row):
    span = r.shape[0]
    row = lax.broadcasted_iota(jnp.int32, (span, span), 0)
    col = lax.broadcasted_iota(jnp.int32, (span, span), 1)
    tril = jnp.where(row >= col, 1.0, 0.0).astype(BF16)
    cum = mm_exact_left(tril, ld)
    mid = cum[span // 2 - 1 : span // 2]
    end = cum[span - 1 : span]
    ea = jnp.exp(cum - ld - mid)
    er = jnp.exp(cum - mid)
    eb = jnp.exp(mid - cum)
    at = -unit * ea
    rt = r * er
    bt = unit * alpha * eb
    kt = sk * eb
    fresh = jnp.where(seg_col == 0.0, 1.0, 0.0)
    lead = jnp.exp(mid) * fresh
    tail = jnp.exp(end - mid) * jnp.where(seg_col == seg_col[span - 1 : span], 1.0, 0.0)
    through = jnp.exp(end) * fresh[span - 1 : span]
    same = seg_col[:, :span] == seg_row
    strict = same & (row > col)
    incl = same & (row >= col)
    return (at, rt, bt, kt, ea, er, eb, lead, tail, through, strict, incl)


def split_terms(array):
    high = array.astype(BF16)
    return (high, (array - high.astype(F32)).astype(BF16))


def interactions(at, rt, bt, kt, strict, incl):
    span = at.shape[0]
    left_high, left_low = split_terms(jnp.concatenate([at, rt], axis=0))
    right_high, right_low = split_terms(jnp.concatenate([bt, kt], axis=0))
    left_high = halves(left_high)
    left_low = halves(left_low)
    right = jnp.concatenate([right_high, right_high, right_low], axis=1)
    result = []
    for half in range(2):
        left = jnp.concatenate([left_high[half], left_low[half], left_high[half]], axis=1)
        full = mm(left, right, NT)
        result.append(
            (
                jnp.where(strict, full[:span, :span], 0.0),
                jnp.where(strict, full[:span, span:], 0.0),
                jnp.where(incl, full[span:, :span], 0.0),
                jnp.where(incl, full[span:, span:], 0.0),
            )
        )
    return result


def unit_inverse(lower):
    span = lower.shape[0]
    row = lax.broadcasted_iota(jnp.int32, (span, span), 0)
    col = lax.broadcasted_iota(jnp.int32, (span, span), 1)
    size = 1
    differ = row ^ col
    solved = jnp.where(row == col, 1.0, 0.0) + jnp.where(differ == 1, lower, 0.0)
    size = 2
    while size < span:
        part = jnp.where((differ >= size) & (differ < 2 * size), lower, 0.0)
        solved = solved + mm(solved, mm(part, solved))
        size *= 2
    return solved


def forward_body(
    r_ref, kr_ref, vr_ref, du_ref, au_ref, vu_ref, fv_ref, vec_ref, seg_col_ref, seg_row_ref,
    q_ref, y_ref, u0_ref, out_ref, bonus_ref, x_ref, t_ref, o_ref,
):
    vec = vec_ref[...]
    r = r_ref[...]
    sig, ld, alpha, vg, mv, scale, unit, mult, sk = prepared(
        kr_ref[...], vr_ref[...], du_ref[...], au_ref[...], vu_ref[...],
        fv_ref[...].astype(F32), vec,
    )
    at, rt, bt, kt, ea, er, eb, lead, tail, through, strict, incl = scaled_parts(
        r, ld, sk, unit, alpha, seg_col_ref[...], seg_row_ref[0:1]
    )
    span = r.shape[0]
    inter = interactions(at, rt, bt, kt, strict, incl)
    inverse = [unit_inverse(inter[half][0]) for half in range(2)]
    v_half = [part.astype(BF16) for part in halves(mv)]
    av = mm(
        jnp.concatenate([inter[0][1], inter[1][1]], axis=1),
        jnp.concatenate(v_half, axis=0),
    )
    a_in = at * lead
    right = jnp.concatenate([av, a_in], axis=1)
    first = lax.broadcasted_iota(jnp.int32, right.shape, 1) % PAIR < HEAD
    solved = mm(
        jnp.concatenate(inverse, axis=1),
        jnp.concatenate([jnp.where(first, right, 0.0), jnp.where(first, 0.0, right)], axis=0),
    )
    u0 = solved[:, :PAIR]
    y = solved[:, PAIR:]
    uy = solved.astype(BF16)
    zero = jnp.zeros_like(uy)
    zero_half = jnp.zeros_like(v_half[0])
    joined = mm(
        jnp.concatenate([inter[0][2], inter[1][2], inter[0][3], inter[1][3]], axis=1),
        jnp.concatenate(
            [
                jnp.where(first, uy, zero),
                jnp.where(first, zero, uy),
                jnp.concatenate([v_half[0], zero_half], axis=1),
                jnp.concatenate([v_half[1], zero_half], axis=1),
            ],
            axis=0,
        ),
    )
    q_ref[...] = (rt * lead + joined[:, PAIR:]).astype(q_ref.dtype)
    out_ref[...] = joined[:, :PAIR]
    y_ref[...] = y.astype(y_ref.dtype)
    u0_ref[...] = u0
    b_tail = bt * tail
    k_tail = kt * tail
    diag_row = lax.broadcasted_iota(jnp.int32, (PAIR, PAIR), 0)
    diag_col = lax.broadcasted_iota(jnp.int32, (PAIR, PAIR), 1)
    transfer = mm(y, b_tail, TN) + jnp.where(diag_row == diag_col, through, 0.0)
    offset = mm(
        jnp.concatenate([u0, mv], axis=0), jnp.concatenate([b_tail, k_tail], axis=0), TN
    )
    t_ref[0] = compact(transfer)
    o_ref[0] = compact(offset)
    x_ref[0] = jnp.concatenate(inverse, axis=0).astype(x_ref.dtype)
    bonus_ref[...] = head_sums(r * sk * vec[11:12]) * mv


def finish_body(q_ref, out_ref, bonus_ref, s_ref, gate_ref, vec_ref, xhat_ref, rstd_ref, branch_ref):
    vec = vec_ref[...]
    out = out_ref[...] + mm(q_ref[...], spread(s_ref[0]), NT)
    center = out - head_sums(out) * (1.0 / HEAD)
    rstd = lax.rsqrt(head_sums(center * center) * (1.0 / HEAD) + GROUP_EPS)
    xhat = center * rstd
    xhat_ref[...] = xhat
    rstd_ref[...] = rstd
    branch_ref[...] = (
        (xhat * vec[12:13] + vec[13:14] + bonus_ref[...]) * gate_ref[...]
    ).astype(branch_ref.dtype)


def early_body(
    db_ref, gate_ref, xhat_ref, rstd_ref, bonus_ref, q_ref, vec_ref,
    dout_ref, dbg_ref, dgate_ref, gs_ref, gvec_ref,
):
    vec = vec_ref[...]
    d_branch = db_ref[...]
    xhat = xhat_ref[...]
    inner = xhat * vec[12:13] + vec[13:14] + bonus_ref[...]
    dgate_ref[...] = (d_branch * inner).astype(dgate_ref.dtype)
    dbg = d_branch * gate_ref[...]
    dbg_ref[...] = dbg
    dn = dbg * vec[12:13]
    dout = rstd_ref[...] * (
        dn - head_sums(dn) * (1.0 / HEAD) - xhat * (head_sums(dn * xhat) * (1.0 / HEAD))
    )
    dout_ref[...] = dout
    gs_ref[0] = compact(mm(dout, q_ref[...], TN))
    gvec_ref[...] = jnp.zeros_like(gvec_ref)
    gvec_ref[4:5] = jnp.sum(dbg * xhat, axis=0, keepdims=True)
    gvec_ref[5:6] = jnp.sum(dbg, axis=0, keepdims=True)


def late_body(
    r_ref, kr_ref, vr_ref, du_ref, au_ref, vu_ref, fv_ref, vec_ref, seg_col_ref, seg_row_ref,
    x_ref, y_ref, u0_ref, s_ref, g_ref, dout_ref, dbg_ref,
    dr_out, dk_out, dv_out, ddu_out, dau_out, dvu_out, dfv_out, gvec_ref,
):
    vec = vec_ref[...]
    r = r_ref[...]
    kr = kr_ref[...]
    vr = vr_ref[...]
    fv = fv_ref[...].astype(F32)
    sig, ld, alpha, vg, mv, scale, unit, mult, sk = prepared(
        kr, vr, du_ref[...], au_ref[...], vu_ref[...], fv, vec
    )
    at, rt, bt, kt, ea, er, eb, lead, tail, through, strict, incl = scaled_parts(
        r, ld, sk, unit, alpha, seg_col_ref[...], seg_row_ref[0:1]
    )
    span = r.shape[0]
    inter = interactions(at, rt, bt, kt, strict, incl)
    state = spread(s_ref[0])
    grad = spread(g_ref[0])
    u = u0_ref[...] + mm(y_ref[...], state, NT)
    dout = dout_ref[...]
    dout_half = [part.astype(BF16) for part in halves(dout)]
    first_pass = mm(
        jnp.concatenate(
            [
                jnp.concatenate([inter[0][2], inter[0][3]], axis=1),
                jnp.concatenate([inter[1][2], inter[1][3]], axis=1),
            ],
            axis=0,
        ),
        jnp.concatenate(dout_half, axis=0),
        TN,
    )
    b_tail = bt * tail
    k_tail = kt * tail
    from_grad = mm(jnp.concatenate([b_tail, k_tail], axis=0), grad, NT)
    first_pass = first_pass + from_grad
    d_u = first_pass[:span]
    d_mv = first_pass[span:]
    w = mm(x_ref[0], jnp.concatenate(halves(d_u), axis=0), TN)
    w_half = [part.astype(BF16) for part in halves(w)]
    d_mv = d_mv + mm(
        jnp.concatenate([inter[0][1], inter[1][1]], axis=0),
        jnp.concatenate(w_half, axis=0),
        TN,
    )
    uv = jnp.concatenate([u, mv], axis=0).astype(BF16)
    bk = jnp.concatenate([bt, kt], axis=0)
    ar = jnp.concatenate([at, rt], axis=0)
    bk_half = halves(bk)
    ar_half = halves(ar)
    d_inter = []
    mask = jnp.concatenate([strict, strict], axis=1)
    mask = jnp.concatenate([mask, mask], axis=0)
    for half in range(2):
        full = mm(jnp.concatenate([w_half[half], dout_half[half]], axis=0), uv, NT)
        d_inter.append(jnp.where(mask, full, 0.0).astype(BF16))
    diag_b = head_sums(dout * u)
    diag_k = head_sums(dout * mv)
    d_ar = mm(jnp.concatenate(d_inter, axis=1), jnp.concatenate(bk_half, axis=0))
    d_bk = mm(jnp.concatenate(d_inter, axis=0), jnp.concatenate(ar_half, axis=0), TN)
    wd = jnp.concatenate([w, dout], axis=0)
    d_in = mm(wd, state)
    d_tail = mm(uv, grad)
    d_at = d_ar[:span] + d_in[:span] * lead
    d_rt = d_ar[span:] + d_in[span:] * lead
    d_bt = d_bk[:span] + d_tail[:span] * tail
    d_kt = d_bk[span:] + d_tail[span:] * tail
    d_before = at * d_at
    d_cum = rt * d_rt - bt * d_bt - kt * d_kt
    at_end = jnp.sum(b_tail * d_tail[:span] + k_tail * d_tail[span:], axis=0, keepdims=True)
    at_end = at_end + through * jnp.sum(s_ref[0] * g_ref[0], axis=0, keepdims=True)
    row = lax.broadcasted_iota(jnp.int32, (span, span), 0)
    col = lax.broadcasted_iota(jnp.int32, (span, span), 1)
    triu = jnp.where(row <= col, 1.0, 0.0).astype(BF16)
    d_ld = mm_exact_left(triu, d_cum + d_before) - d_before + at_end
    d_r = d_rt * er + diag_b * (unit * alpha) + diag_k * sk
    d_a = d_at * ea
    d_b = d_bt * eb + diag_b * r
    d_sk = d_kt * eb + diag_k * r
    dbg = dbg_ref[...]
    extra = head_sums(r * sk * vec[11:12])
    d_extra = head_sums(dbg * mv)
    d_mv = d_mv + dbg * extra
    d_r = d_r + d_extra * sk * vec[11:12]
    d_sk = d_sk + d_extra * r * vec[11:12]
    d_unit = d_b * alpha - d_a
    d_alpha = d_b * unit + d_sk * kr * vec[10:11]
    d_raw = scale * (d_unit - unit * head_sums(d_unit * unit))
    d_kr = d_raw * vec[9:10] + d_sk * mult
    d_du = d_ld * ld * (1.0 - sig)
    d_au = d_alpha * alpha * (1.0 - alpha)
    d_vg = d_mv * (fv - vr)
    d_vu = d_vg * vg * (1.0 - vg)
    dr_out[...] = d_r.astype(dr_out.dtype)
    dk_out[...] = d_kr.astype(dk_out.dtype)
    dv_out[...] = (d_mv * (1.0 - vg)).astype(dv_out.dtype)
    ddu_out[...] = d_du.astype(ddu_out.dtype)
    dau_out[...] = d_au.astype(dau_out.dtype)
    dvu_out[...] = d_vu.astype(dvu_out.dtype)
    dfv_out[...] = d_mv * vg
    gvec_ref[...] = jnp.zeros_like(gvec_ref)
    gvec_ref[0:1] = jnp.sum(d_du, axis=0, keepdims=True)
    gvec_ref[1:2] = jnp.sum(d_au, axis=0, keepdims=True)
    gvec_ref[2:3] = jnp.sum(d_vu, axis=0, keepdims=True)
    gvec_ref[3:4] = jnp.sum(d_raw * kr, axis=0, keepdims=True)
    gvec_ref[4:5] = jnp.sum(d_sk * kr * (alpha - 1.0), axis=0, keepdims=True)
    gvec_ref[5:6] = jnp.sum(d_extra * r * sk, axis=0, keepdims=True)


def merge_body(old_o_ref, old_t_ref, o_ref, t_ref, new_o_ref, new_t_ref):
    for pair in range(o_ref.shape[0]):
        both = jnp.concatenate([old_o_ref[pair], old_t_ref[pair]], axis=0)
        moved = mm(both, spread(t_ref[pair]))
        new_o_ref[pair] = o_ref[pair] + moved[:HEAD]
        new_t_ref[pair] = moved[HEAD:].astype(new_t_ref.dtype)


def merge_last_body(old_o_ref, o_ref, t_ref, new_o_ref):
    for pair in range(o_ref.shape[0]):
        new_o_ref[pair] = o_ref[pair] + mm(old_o_ref[pair], spread(t_ref[pair]))


def merge_back_body(next_g_ref, g_ref, t_ref, new_g_ref):
    for pair in range(g_ref.shape[0]):
        new_g_ref[pair] = g_ref[pair] + mm(next_g_ref[pair], spread(t_ref[pair]), NT)


def cols(span):
    return pl.BlockSpec((span, PAIR), lambda pair: (0, pair))


def per_pair(rows):
    return pl.BlockSpec((1, rows, PAIR), lambda pair: (pair, 0, 0))


def fixed(shape):
    return pl.BlockSpec(shape, lambda pair: (0,) * len(shape))


def shaped(shape, dtype):
    return jax.ShapeDtypeStruct(shape, dtype)


def forward_call(raws, fv, vec, seg_col, seg_row):
    span, width = fv.shape
    pairs = width // PAIR
    return pl.pallas_call(
        forward_body,
        grid=(pairs,),
        in_specs=[cols(span)] * 7 + [cols(vec.shape[0]), fixed(seg_col.shape), fixed(seg_row.shape)],
        out_specs=[cols(span)] * 5 + [per_pair(2 * span), per_pair(HEAD), per_pair(HEAD)],
        out_shape=[
            shaped((span, width), BF16),
            shaped((span, width), BF16),
            shaped((span, width), F32),
            shaped((span, width), F32),
            shaped((span, width), F32),
            shaped((pairs, 2 * span, span), BF16),
            shaped((pairs, HEAD, PAIR), F32),
            shaped((pairs, HEAD, PAIR), F32),
        ],
        name="wkv_forward",
    )(*raws, fv, vec, seg_col, seg_row)


def finish_call(q, out, bonus, state, gate, vec):
    span, width = out.shape
    return pl.pallas_call(
        finish_body,
        grid=(width // PAIR,),
        in_specs=[cols(span)] * 3 + [per_pair(HEAD), cols(span), cols(vec.shape[0])],
        out_specs=[cols(span)] * 3,
        out_shape=[
            shaped((span, width), F32), shaped((span, width), F32), shaped((span, width), BF16),
        ],
        name="wkv_finish",
    )(q, out, bonus, state, gate, vec)


def early_call(d_branch, gate, xhat, rstd, bonus, q, vec):
    span, width = xhat.shape
    pairs = width // PAIR
    return pl.pallas_call(
        early_body,
        grid=(pairs,),
        in_specs=[cols(span)] * 6 + [cols(vec.shape[0])],
        out_specs=[cols(span)] * 3 + [per_pair(HEAD), cols(8)],
        out_shape=[
            shaped((span, width), F32),
            shaped((span, width), F32),
            shaped((span, width), BF16),
            shaped((pairs, HEAD, PAIR), F32),
            shaped((8, width), F32),
        ],
        name="wkv_early",
    )(d_branch, gate, xhat, rstd, bonus, q, vec)


def late_call(raws, fv, vec, seg_col, seg_row, x, y, u0, state, grad, dout, dbg):
    span, width = fv.shape
    pairs = width // PAIR
    return pl.pallas_call(
        late_body,
        grid=(pairs,),
        in_specs=[cols(span)] * 7
        + [cols(vec.shape[0]), fixed(seg_col.shape), fixed(seg_row.shape)]
        + [per_pair(2 * span), cols(span), cols(span), per_pair(HEAD), per_pair(HEAD)]
        + [cols(span)] * 2,
        out_specs=[cols(span)] * 7 + [cols(8)],
        out_shape=[shaped((span, width), BF16)] * 6
        + [shaped((span, width), F32), shaped((8, width), F32)],
        name="wkv_late",
    )(*raws, fv, vec, seg_col, seg_row, x, y, u0, state, grad, dout, dbg)


def merge_call(old_o, old_t, o, t):
    return pl.pallas_call(
        merge_body,
        out_shape=[shaped(o.shape, F32), shaped(o.shape, BF16)],
        name="state_merge",
    )(old_o, old_t, o, t)


def merge_last_call(old_o, o, t):
    return pl.pallas_call(
        merge_last_body, out_shape=shaped(o.shape, F32), name="state_merge_last"
    )(old_o, o, t)


def merge_back_call(next_g, g, t):
    return pl.pallas_call(
        merge_back_body, out_shape=shaped(g.shape, F32), name="state_merge_back"
    )(next_g, g, t)


def matmul(left, right):
    return jnp.dot(left, right, preferred_element_type=F32)


def matmul_nt(left, right):
    return lax.dot_general(left, right, NT, preferred_element_type=F32)


def matmul_tn(left, right):
    return lax.dot_general(left, right, TN, preferred_element_type=F32)


def layer_norm(values, gain, bias_row):
    center = values - jnp.mean(values, axis=-1, keepdims=True)
    spread_sq = jnp.mean(center * center, axis=-1, keepdims=True)
    return center * lax.rsqrt(spread_sq + LN_EPS) * gain + bias_row


def blend_rows(current, earlier, keep_row, gain_rows):
    change = earlier * keep_row - current
    return current[None] + change[None] * gain_rows[:, None, :]


def shifted(value, steps):
    count = lax.axis_size("seq")
    initial, last = (max(0, -steps), min(count, count - steps))
    return lax.ppermute(value, "seq", [(place, place + steps) for place in range(initial, last)])


def partner(value, axis, flip):
    count = lax.axis_size(axis)
    return lax.ppermute(value, axis, [(place, place ^ flip) for place in range(count)])


def after(value, *others):
    return lax.optimization_barrier((value,) + others)[0]


def gather_blocks(shard):
    count = lax.axis_size("fsdp")
    copies = jnp.broadcast_to(shard[None], (count,) + shard.shape)
    return lax.all_to_all(copies, "fsdp", split_axis=0, concat_axis=0, tiled=True)


def gather_weight(shard, axis, core):
    size = shard.shape[axis] // 2
    half = lax.dynamic_slice_in_dim(shard, core * size, size, axis)
    mine = gather_blocks(half)
    other = partner(mine, "seq", 1)
    low = jnp.where(core == 0, mine, other)
    high = jnp.where(core == 0, other, mine)
    return jnp.concatenate([low, high], axis=axis + 1)


def gather_rows(rows):
    count = lax.axis_size("fsdp")
    pieces = [rows] + [partner(rows, "fsdp", flip) for flip in range(1, count)]
    return jnp.concatenate(pieces, axis=0)


def scatter_rows(rows):
    count = lax.axis_size("fsdp")
    size = rows.shape[0] // count
    total = rows[:size].astype(F32)
    for flip in range(1, count):
        total = total + partner(rows[flip * size : (flip + 1) * size], "fsdp", flip).astype(F32)
    return total


def columns_to_owner(array):
    return lax.all_to_all(array, "fsdp", split_axis=array.ndim - 1, concat_axis=array.ndim - 2, tiled=True)


def reduce_seq(array):
    count = lax.axis_size("seq")
    chips = count // 2
    place = lax.axis_index("seq")
    core = place % 2
    chip = place // 2
    half = array.shape[0] // 2
    part = half // chips
    own = lax.dynamic_slice_in_dim(array, core * half, half, 0)
    other = partner(lax.dynamic_slice_in_dim(array, (1 - core) * half, half, 0), "seq", 1)
    on_chip = (own.astype(F32) + other.astype(F32)).astype(BF16).reshape(chips, part, -1)
    total = lax.dynamic_index_in_dim(on_chip, chip, 0, False).astype(F32)
    for flip in range(1, chips):
        leaving = lax.dynamic_index_in_dim(on_chip, chip ^ flip, 0, False)
        total = total + partner(leaving, "seq", 2 * flip).astype(F32)
    total = total.astype(BF16)
    pieces = jnp.zeros(on_chip.shape, BF16)
    pieces = lax.dynamic_update_index_in_dim(pieces, total, chip, 0)
    for flip in range(1, chips):
        pieces = lax.dynamic_update_index_in_dim(
            pieces, partner(total, "seq", 2 * flip), chip ^ flip, 0
        )
    mine = pieces.reshape(half, -1)
    other = partner(mine, "seq", 1)
    low = jnp.where(core == 0, mine, other)
    high = jnp.where(core == 0, other, mine)
    return jnp.concatenate([low, high], axis=0).astype(F32)


def by_core(core, mine, other):
    return (jnp.where(core == 0, mine, other), jnp.where(core == 0, other, mine))


def own_pairs(core, array):
    size = array.shape[0] // 2
    return lax.dynamic_slice_in_dim(array, core * size, size, 0)


def all_pairs(core, mine):
    low, high = by_core(core, mine, partner(mine, "seq", 1))
    return jnp.concatenate([low, high], axis=0)


def body(
    layer_input,
    first_layer_values,
    document_numbers,
    output_cotangent,
    projection_matrices,
    time_output_matrix,
    lowrank_first,
    lowrank_second,
    channel_key_matrix,
    channel_value_matrix,
    vectors,
):
    groups = lax.axis_size("fsdp")
    place = lax.axis_index("seq")
    core = place % 2
    chips = lax.axis_size("seq") // 2
    span, width = layer_input.shape[1:]
    resid_in = layer_input[0].astype(F32)
    first_values = first_layer_values[0]
    cotangent = output_cotangent[0]
    id_plus = document_numbers[0].astype(F32) + 1.0

    edge = jnp.concatenate(
        [resid_in[span - 1 :], jnp.broadcast_to(id_plus[span - 1 :, None], (1, PAIR))], axis=1
    )
    edge = shifted(edge, 1)
    vec_blocks = gather_blocks(vectors)
    down_blocks = gather_weight(lowrank_first, 0, core)
    second_blocks = gather_weight(lowrank_second, 0, core)
    proj_blocks = gather_weight(after(projection_matrices, down_blocks, second_blocks), 1, core)
    out_blocks = gather_weight(after(time_output_matrix, proj_blocks), 0, core)
    cot_rows = gather_rows(after(cotangent, out_blocks))

    vec = jnp.swapaxes(vec_blocks, 0, 1).reshape(-1, width).astype(F32)
    down = down_blocks.reshape(width, -1)
    second = jnp.swapaxes(second_blocks, 0, 1).reshape(-1, width)
    out_full = out_blocks.reshape(width, width)
    down_parts = [down[:, BOUNDS[part] : BOUNDS[part + 1]] for part in range(4)]
    second_parts = [second[BOUNDS[part] : BOUNDS[part + 1]] for part in range(4)]
    vec_rows = jnp.concatenate([vec, jnp.zeros((24 - vec.shape[0], width), F32)], axis=0)

    edge_id = edge[0, width]
    earlier_ids = jnp.concatenate([edge[0, width : width + 1], id_plus[:-1]])
    keep_row = (id_plus == earlier_ids).astype(F32)[:, None]
    segment = id_plus - edge_id
    seg_col = jnp.broadcast_to(segment[:, None], (span, PAIR))
    seg_row = jnp.broadcast_to(segment[None], (8, span))

    def mixer(current, earlier, gain_rows):
        return blend_rows(current, earlier, keep_row, gain_rows)

    normed_one, ln_one_back = jax.vjp(layer_norm, resid_in, vec[14], vec[15])
    edge_row = layer_norm(edge[:, :width], vec[14], vec[15])
    earlier_one = jnp.concatenate([edge_row, normed_one[:-1]])
    mixed_rows, mix_back = jax.vjp(mixer, normed_one, earlier_one, vec[0:6])
    mixed = mixed_rows.astype(BF16)
    decay_pre = matmul(mixed[1], down_parts[0])
    low_decay = jnp.tanh(decay_pre).astype(BF16)
    low_alpha = matmul(mixed[4], down_parts[1]).astype(BF16)
    low_vmix = matmul(mixed[3], down_parts[2]).astype(BF16)
    gate_pre = matmul(mixed[5], down_parts[3])
    low_gate = jax.nn.sigmoid(gate_pre).astype(BF16)
    lows = (low_decay, low_alpha, low_vmix, low_gate)
    decay_up, alpha_up, vmix_up, gate = [
        matmul(lows[part], second_parts[part]) for part in range(4)
    ]
    mix_three = (mixed[0], mixed[2], mixed[3])
    recept, key_raw, value_raw = [
        jnp.concatenate(
            [matmul(mix_three[part], proj_blocks[block, part]) for block in range(groups)], axis=1
        )
        for part in range(3)
    ]
    raws = (recept, key_raw, value_raw, decay_up, alpha_up, vmix_up)
    query, y_part, u_part, out_part, bonus, inverse, transfer, offset = forward_call(
        raws, first_values, vec_rows, seg_col, seg_row
    )
    mix_rows = lax.all_gather(
        after(jnp.stack(mix_three), cot_rows), "fsdp", axis=1, tiled=True
    )

    transfer_b = transfer.astype(BF16)
    both = jnp.concatenate([offset.astype(BF16), transfer_b], axis=0)
    other = partner(both, "seq", 1)
    pairs = offset.shape[0]
    other_offset, other_transfer = (other[:pairs], other[pairs:])
    offset_zero, offset_one = by_core(core, offset, other_offset.astype(F32))
    transfer_zero, transfer_one = by_core(core, transfer_b, other_transfer)
    chip_offset, chip_transfer = merge_call(
        own_pairs(core, offset_zero),
        own_pairs(core, transfer_zero),
        own_pairs(core, offset_one),
        own_pairs(core, transfer_one),
    )
    arriving = shifted(chip_offset.astype(BF16), 2)
    for _ in range(chips - 2):
        arriving = shifted(
            merge_last_call(arriving, chip_offset, chip_transfer).astype(BF16), 2
        )
    chip_state = all_pairs(core, arriving).astype(F32)
    state = jnp.where(
        core == 0, chip_state, merge_last_call(chip_state, offset_zero, transfer_zero)
    )

    xhat, rstd, branch = finish_call(query, out_part, bonus, state, gate, vec_rows)
    middle = resid_in + matmul(branch, out_full)
    normed_two, ln_two_back = jax.vjp(layer_norm, middle, vec[16], vec[17])
    edge_two = shifted(normed_two[span - 1 :], 1)
    earlier_two = jnp.concatenate([edge_two, normed_two[:-1]])
    cmix_in, cmix_back = jax.vjp(mixer, normed_two, earlier_two, vec[18:19])
    cmix_rows = gather_rows(cmix_in[0].astype(BF16))
    pre_act = matmul(cmix_rows, channel_key_matrix)
    d_hidden = matmul_nt(cot_rows, channel_value_matrix)
    active = jax.nn.relu(pre_act)
    hidden = jnp.square(active).astype(BF16)
    d_pre = (d_hidden * 2.0 * active).astype(BF16)
    d_cmix = scatter_rows(matmul_nt(d_pre, channel_key_matrix).astype(BF16))
    block_out = (
        middle + scatter_rows(after(matmul(hidden, channel_value_matrix).astype(BF16), d_cmix))
    ).astype(BF16)
    grad_value = matmul_tn(hidden, cot_rows)
    grad_key = matmul_tn(cmix_rows, d_pre)
    grad_value, grad_key = [
        part.astype(F32)
        for part in lax.psum((grad_value.astype(BF16), grad_key.astype(BF16)), "seq")
    ]

    d_normed_two, d_earlier_two, d_cmix_gain = cmix_back(d_cmix[None])
    back_two = shifted(d_earlier_two[:1], -1)
    d_middle, d_gain_two, d_bias_two = ln_two_back(
        d_normed_two + jnp.concatenate([d_earlier_two[1:], back_two])
    )
    d_middle = d_middle + cotangent.astype(F32)
    d_middle_b = d_middle.astype(BF16)
    d_branch = matmul_nt(d_middle_b, out_full)
    d_out, d_inner, d_gate, start_grad, vec_early = early_call(
        d_branch, gate, xhat, rstd, bonus, query, vec_rows
    )

    other_start = partner(start_grad.astype(BF16), "seq", 1).astype(F32)
    start_zero, start_one = by_core(core, start_grad, other_start)
    chip_start = merge_back_call(
        own_pairs(core, start_one), own_pairs(core, start_zero), own_pairs(core, transfer_zero)
    )
    arriving = shifted(chip_start.astype(BF16), -2)
    for _ in range(chips - 2):
        arriving = shifted(
            merge_back_call(arriving, chip_start, chip_transfer).astype(BF16), -2
        )
    chip_end = all_pairs(core, arriving).astype(F32)
    end_grad = jnp.where(
        core == 0, merge_back_call(chip_end, start_one, transfer_one), chip_end
    )

    d_recept, d_key, d_value, d_decay, d_alpha, d_vmix, d_first, vec_late = late_call(
        raws, first_values, vec_rows, seg_col, seg_row,
        inverse, y_part, u_part, state, end_grad, d_out, d_inner,
    )

    branch_cols = columns_to_owner(after(branch, d_cmix))
    d_middle_rows = lax.all_gather(d_middle_b, "fsdp", axis=0, tiled=True)
    grad_out = reduce_seq(matmul_tn(branch_cols, d_middle_rows).astype(BF16))

    head_grads = columns_to_owner(jnp.stack([d_recept, d_key, d_value]))
    grad_proj = jnp.concatenate(
        [matmul_tn(mix_rows[part], head_grads[part]) for part in range(3)], axis=0
    ).astype(BF16)

    ups = (d_decay, d_alpha, d_vmix, d_gate)
    grad_up = jnp.concatenate([matmul_tn(lows[part], ups[part]) for part in range(4)], axis=0)
    d_lows = [matmul_nt(ups[part], second_parts[part]) for part in range(4)]
    tanh_now = jnp.tanh(decay_pre)
    sigma_now = jax.nn.sigmoid(gate_pre)
    low_grads = (
        (d_lows[0] * (1.0 - tanh_now * tanh_now)).astype(BF16),
        d_lows[1].astype(BF16),
        d_lows[2].astype(BF16),
        (d_lows[3] * sigma_now * (1.0 - sigma_now)).astype(BF16),
    )
    low_mixes = (mixed[1], mixed[4], mixed[3], mixed[5])
    grad_down = jnp.concatenate(
        [matmul_tn(low_grads[part], low_mixes[part]) for part in range(4)], axis=0
    )
    wide = jnp.moveaxis(proj_blocks, 0, 2).reshape(3, width, width)
    d_mixed = jnp.stack(
        [
            matmul_nt(d_recept, wide[0]),
            matmul_nt(low_grads[0], down_parts[0]),
            matmul_nt(d_key, wide[1]),
            matmul_nt(d_value, wide[2]) + matmul_nt(low_grads[2], down_parts[2]),
            matmul_nt(low_grads[1], down_parts[1]),
            matmul_nt(low_grads[3], down_parts[3]),
        ]
    )
    d_normed_one, d_earlier_one, d_mix_gains = mix_back(d_mixed)
    back_one = shifted(d_earlier_one[:1], -1)
    d_resid, d_gain_one, d_bias_one = ln_one_back(
        d_normed_one + jnp.concatenate([d_earlier_one[1:], back_one])
    )
    d_input = d_resid + d_middle

    grad_vec = jnp.concatenate(
        [
            d_mix_gains,
            vec_late[0:6],
            vec_early[4:6],
            d_gain_one[None],
            d_bias_one[None],
            d_gain_two[None],
            d_bias_two[None],
            d_cmix_gain,
        ],
        axis=0,
    )
    small = jnp.concatenate([grad_up, grad_down, grad_vec], axis=0).astype(BF16)
    block = 2 * 16 * chips
    rows = 3 * width + small.shape[0]
    fill = -rows % block
    small = jnp.concatenate([small, jnp.zeros((fill, width), BF16)], axis=0)
    small_cols = columns_to_owner(small[:, None]).astype(F32)
    small_own = jnp.sum(small_cols, axis=1).astype(BF16)
    total = reduce_seq(jnp.concatenate([grad_proj, small_own], axis=0))
    base = 3 * width
    inner = BOUNDS[4]
    return (
        block_out[None],
        d_input[None],
        d_first[None],
        total[:base].reshape(3, width, -1),
        grad_out,
        total[base + inner : base + 2 * inner].T,
        total[base : base + inner],
        grad_key,
        grad_value,
        total[base + 2 * inner : base + 2 * inner + vectors.shape[0]],
    )


def solution(mesh):
    in_specs = (
        P("fsdp", "seq", None),
        P("fsdp", "seq", None),
        P("fsdp", "seq"),
        P("fsdp", "seq", None),
        P(None, None, "fsdp"),
        P("fsdp", None),
        P("fsdp", None),
        P(None, "fsdp"),
        P(None, "fsdp"),
        P("fsdp", None),
        P(None, "fsdp"),
    )
    out_specs = (
        P("fsdp", "seq", None),
        P("fsdp", "seq", None),
        P("fsdp", "seq", None),
        P(None, None, "fsdp"),
        P("fsdp", None),
        P("fsdp", None),
        P(None, "fsdp"),
        P(None, "fsdp"),
        P("fsdp", None),
        P(None, "fsdp"),
    )
    return jax.shard_map(body, mesh=mesh, in_specs=in_specs, out_specs=out_specs, check_vma=False)
```

```python
import jax
import jax.numpy as jnp
from jax import lax
from jax.experimental import pallas as pl
from jax.experimental.pallas import tpu as pltpu
from jax.sharding import PartitionSpec as P

F32 = jnp.float32
BF16 = jnp.bfloat16
HEAD = 64
PAIR = 128
BLOCK = 256
BOUNDS = (0, 64, 128, 160, 288)
LN_EPS = 1e-05
GROUP_EPS = 0.00064
UNIT_EPS = 1e-06
NN = (((1,), (0,)), ((), ()))
NT = (((1,), (1,)), ((), ()))
TN = (((0,), (0,)), ((), ()))


def mm(left, right, dims=NN):
    return lax.dot_general(
        left.astype(BF16), right.astype(BF16), dims, preferred_element_type=F32
    )


def mm_exact_left(left, right, dims=NN):
    high = right.astype(BF16)
    low = (right - high.astype(F32)).astype(BF16)
    return lax.dot_general(left, high, dims, preferred_element_type=F32) + lax.dot_general(
        left, low, dims, preferred_element_type=F32
    )


def mm_exact_right(left, right):
    high = left.astype(BF16)
    low = (left - high.astype(F32)).astype(BF16)
    return lax.dot_general(high, right, NN, preferred_element_type=F32) + lax.dot_general(
        low, right, NN, preferred_element_type=F32
    )


def lane_halves(shape):
    lane = lax.broadcasted_iota(jnp.int32, shape, 1)
    return lane < HEAD


def halves(array):
    first = lane_halves(array.shape)
    zero = jnp.zeros_like(array)
    return (jnp.where(first, array, zero), jnp.where(first, zero, array))


def head_sums(array):
    row = lax.broadcasted_iota(jnp.int32, (PAIR, PAIR), 0)
    col = lax.broadcasted_iota(jnp.int32, (PAIR, PAIR), 1)
    ones = jnp.where((row < HEAD) == (col < HEAD), 1.0, 0.0).astype(BF16)
    return mm_exact_right(array, ones)


def compact(block):
    return jnp.where(lane_halves((HEAD, PAIR)), block[:HEAD], block[HEAD:])


def spread(pair):
    return jnp.concatenate(halves(pair), axis=0)


def prepared(kr, vr, du, au, vu, fv, vec):
    decay_in = vec[6:7] + du
    sig = jax.nn.sigmoid(decay_in)
    ld = sig * (-0.6065306597126334)
    alpha = jax.nn.sigmoid(vec[7:8] + au)
    vg = jax.nn.sigmoid(vec[8:9] + vu)
    mv = vr + (fv - vr) * vg
    raw_unit = kr * vec[9:10]
    scale = lax.rsqrt(head_sums(raw_unit * raw_unit) + UNIT_EPS)
    unit = raw_unit * scale
    mult = 1.0 + (alpha - 1.0) * vec[10:11]
    sk = kr * mult
    return (sig, ld, alpha, vg, mv, scale, unit, mult, sk)


def scaled_parts(r, ld, sk, unit, alpha, seg_col, seg_row):
    span = r.shape[0]
    row = lax.broadcasted_iota(jnp.int32, (span, span), 0)
    col = lax.broadcasted_iota(jnp.int32, (span, span), 1)
    tril = jnp.where(row >= col, 1.0, 0.0).astype(BF16)
    cum = mm_exact_left(tril, ld)
    mid = cum[span // 2 - 1 : span // 2]
    end = cum[span - 1 : span]
    ea = jnp.exp(cum - ld - mid)
    er = jnp.exp(cum - mid)
    eb = jnp.exp(mid - cum)
    at = -unit * ea
    rt = r * er
    bt = unit * alpha * eb
    kt = sk * eb
    fresh = jnp.where(seg_col == 0.0, 1.0, 0.0)
    lead = jnp.exp(mid) * fresh
    tail = jnp.exp(end - mid) * jnp.where(seg_col == seg_col[span - 1 : span], 1.0, 0.0)
    through = jnp.exp(end) * fresh[span - 1 : span]
    same = seg_col[:, :span] == seg_row
    strict = same & (row > col)
    incl = same & (row >= col)
    return (at, rt, bt, kt, ea, er, eb, lead, tail, through, strict, incl)


def split_terms(array):
    high = array.astype(BF16)
    return (high, (array - high.astype(F32)).astype(BF16))


def interactions(at, rt, bt, kt, strict, incl):
    span = at.shape[0]
    left_high, left_low = split_terms(jnp.concatenate([at, rt], axis=0))
    right_high, right_low = split_terms(jnp.concatenate([bt, kt], axis=0))
    left_high = halves(left_high)
    left_low = halves(left_low)
    right = jnp.concatenate([right_high, right_high, right_low], axis=1)
    result = []
    for half in range(2):
        left = jnp.concatenate([left_high[half], left_low[half], left_high[half]], axis=1)
        full = mm(left, right, NT)
        result.append(
            (
                jnp.where(strict, full[:span, :span], 0.0),
                jnp.where(strict, full[:span, span:], 0.0),
                jnp.where(incl, full[span:, :span], 0.0),
                jnp.where(incl, full[span:, span:], 0.0),
            )
        )
    return result


def unit_inverses(lowers):
    span = lowers[0].shape[0]
    row = lax.broadcasted_iota(jnp.int32, (span, span), 0)
    col = lax.broadcasted_iota(jnp.int32, (span, span), 1)
    differ = row ^ col
    eye = jnp.where(row == col, 1.0, 0.0)
    solved = [eye + jnp.where(differ == 1, lower, 0.0) for lower in lowers]
    size = 2
    while size < span:
        between = (differ >= size) & (differ < 2 * size)
        parts = [jnp.where(between, lower, 0.0) for lower in lowers]
        inner = [mm(part, done) for part, done in zip(parts, solved)]
        solved = [done + mm(done, part) for done, part in zip(solved, inner)]
        size *= 2
    return solved


def forward_body(
    mine_mix_ref, other_mix_ref, mine_ref, other_ref,
    low0_ref, low1_ref, low2_ref, low3_ref, second_ref,
    fv_ref, vec_ref, seg_col_ref, seg_row_ref, *refs
):
    outs = refs[len(refs) - 14 :]
    raw_refs = outs[0:6]
    gate_ref, q_ref, y_ref, u0_ref, out_ref, bonus_ref, x_ref, both_ref = outs[6:]
    for part in range(3):
        raw_refs[part][...] = mm(mine_mix_ref[part], mine_ref[part]) + mm(
            other_mix_ref[part], other_ref[part]
        )
    lows = (low0_ref, low1_ref, low2_ref, low3_ref)
    for part in range(4):
        target = raw_refs[3 + part] if part < 3 else gate_ref
        target[...] = mm(lows[part][...], second_ref[BOUNDS[part] : BOUNDS[part + 1]])
    count = fv_ref.shape[1] // PAIR
    early = []
    for pair in range(count):
        lanes = slice(pair * PAIR, (pair + 1) * PAIR)
        vec = vec_ref[:, lanes]
        r, kr, vr, du, au, vu = [ref[:, lanes] for ref in raw_refs]
        sig, ld, alpha, vg, mv, scale, unit, mult, sk = prepared(
            kr, vr, du, au, vu, fv_ref[:, lanes].astype(F32), vec
        )
        at, rt, bt, kt, ea, er, eb, lead, tail, through, strict, incl = scaled_parts(
            r, ld, sk, unit, alpha, seg_col_ref[...], seg_row_ref[0:1]
        )
        inter = interactions(at, rt, bt, kt, strict, incl)
        bonus_ref[:, lanes] = head_sums(r * sk * vec[11:12]) * mv
        early.append((mv, at * lead, rt * lead, bt * tail, kt * tail, through, inter))
    found = unit_inverses([item[6][half][0] for item in early for half in range(2)])
    for pair in range(count):
        lanes = slice(pair * PAIR, (pair + 1) * PAIR)
        mv, a_in, r_in, b_tail, k_tail, through, inter = early[pair]
        inverse = found[2 * pair : 2 * pair + 2]
        v_half = [part.astype(BF16) for part in halves(mv)]
        av = mm(
            jnp.concatenate([inter[0][1], inter[1][1]], axis=1),
            jnp.concatenate(v_half, axis=0),
        )
        right = jnp.concatenate([av, a_in], axis=1)
        first = lax.broadcasted_iota(jnp.int32, right.shape, 1) % PAIR < HEAD
        solved = mm(
            jnp.concatenate(inverse, axis=1),
            jnp.concatenate([jnp.where(first, right, 0.0), jnp.where(first, 0.0, right)], axis=0),
        )
        u0 = solved[:, :PAIR]
        y = solved[:, PAIR:]
        uy = solved.astype(BF16)
        zero = jnp.zeros_like(uy)
        zero_half = jnp.zeros_like(v_half[0])
        joined = mm(
            jnp.concatenate([inter[0][2], inter[1][2], inter[0][3], inter[1][3]], axis=1),
            jnp.concatenate(
                [
                    jnp.where(first, uy, zero),
                    jnp.where(first, zero, uy),
                    jnp.concatenate([v_half[0], zero_half], axis=1),
                    jnp.concatenate([v_half[1], zero_half], axis=1),
                ],
                axis=0,
            ),
        )
        q_ref[:, lanes] = (r_in + joined[:, PAIR:]).astype(q_ref.dtype)
        out_ref[:, lanes] = joined[:, :PAIR]
        y_ref[:, lanes] = y.astype(y_ref.dtype)
        u0_ref[:, lanes] = u0
        diag_row = lax.broadcasted_iota(jnp.int32, (PAIR, PAIR), 0)
        diag_col = lax.broadcasted_iota(jnp.int32, (PAIR, PAIR), 1)
        transfer = mm(y, b_tail, TN) + jnp.where(diag_row == diag_col, through, 0.0)
        offset = mm(
            jnp.concatenate([u0, mv], axis=0), jnp.concatenate([b_tail, k_tail], axis=0), TN
        )
        both_ref[0, pair] = compact(offset).astype(both_ref.dtype)
        both_ref[1, pair] = compact(transfer).astype(both_ref.dtype)
        x_ref[pair] = jnp.concatenate(inverse, axis=0).astype(x_ref.dtype)


def finish_body(q_ref, out_ref, bonus_ref, s_ref, gate_ref, vec_ref, xhat_ref, rstd_ref, branch_ref):
    for pair in range(out_ref.shape[1] // PAIR):
        lanes = slice(pair * PAIR, (pair + 1) * PAIR)
        vec = vec_ref[:, lanes]
        out = out_ref[:, lanes] + mm(q_ref[:, lanes], spread(s_ref[pair]), NT)
        center = out - head_sums(out) * (1.0 / HEAD)
        rstd = lax.rsqrt(head_sums(center * center) * (1.0 / HEAD) + GROUP_EPS)
        xhat = center * rstd
        xhat_ref[:, lanes] = xhat
        rstd_ref[:, lanes] = rstd
        branch_ref[:, lanes] = (
            (xhat * vec[12:13] + vec[13:14] + bonus_ref[:, lanes]) * gate_ref[:, lanes]
        ).astype(branch_ref.dtype)


def early_body(
    db_ref, gate_ref, xhat_ref, rstd_ref, bonus_ref, q_ref, vec_ref,
    dout_ref, dbg_ref, dgate_ref, gs_ref, gvec_ref,
):
    gvec_ref[...] = jnp.zeros_like(gvec_ref)
    for pair in range(db_ref.shape[1] // PAIR):
        lanes = slice(pair * PAIR, (pair + 1) * PAIR)
        vec = vec_ref[:, lanes]
        d_branch = db_ref[:, lanes]
        xhat = xhat_ref[:, lanes]
        inner = xhat * vec[12:13] + vec[13:14] + bonus_ref[:, lanes]
        dgate_ref[:, lanes] = (d_branch * inner).astype(dgate_ref.dtype)
        dbg = d_branch * gate_ref[:, lanes]
        dbg_ref[:, lanes] = dbg
        dn = dbg * vec[12:13]
        dout = rstd_ref[:, lanes] * (
            dn - head_sums(dn) * (1.0 / HEAD) - xhat * (head_sums(dn * xhat) * (1.0 / HEAD))
        )
        dout_ref[:, lanes] = dout
        gs_ref[pair] = compact(mm(dout, q_ref[:, lanes], TN)).astype(gs_ref.dtype)
        gvec_ref[0:1, lanes] = jnp.sum(dbg * xhat, axis=0, keepdims=True)
        gvec_ref[1:2, lanes] = jnp.sum(dbg, axis=0, keepdims=True)


def late_body(
    r_ref, kr_ref, vr_ref, du_ref, au_ref, vu_ref, fv_ref, vec_ref, seg_col_ref, seg_row_ref,
    x_ref, y_ref, u0_ref, s_ref, g_ref, dout_ref, dbg_ref, dgate_ref,
    early_ref, second_ref, low0_ref, low1_ref, low2_ref, low3_ref, *refs
):
    gvec_ref, weight_ref, sem = refs[len(refs) - 3 :]
    outs = refs[len(refs) - 12 : len(refs) - 3]
    sources = refs[: len(refs) - 12]
    pieces = len(sources) // 2
    three_ref, dfv_out, up_out = outs[:3]
    mine_out, other_out, l0_out, l1_out, l2_out, l3_out = outs[3:]
    step = pl.program_id(0)
    each = sources[0].shape[2] // BLOCK

    def copies(base, at):
        found = []
        for side in range(2):
            source = sources[2 * base + side]
            if each > 1:
                source = source.at[:, :, pl.ds(pl.multiple_of(at * BLOCK, BLOCK), BLOCK)]
            found.append(
                pltpu.make_async_copy(source, weight_ref.at[at % 2, side], sem.at[at % 2, side])
            )
        return found

    @pl.when(step == 0)
    def fetch_first():
        for copy in copies(0, step):
            copy.start()

    for base in range(pieces):

        @pl.when(((step + 1) // each == base) & (step + 1 < pl.num_programs(0)))
        def fetch(base=base):
            for copy in copies(base, step + 1):
                copy.start()

    places = {0: mine_out, 1: other_out, 2: l0_out, 3: l1_out, 4: l2_out, 5: l3_out}
    gvec_ref[...] = jnp.zeros_like(gvec_ref)
    count = fv_ref.shape[1] // PAIR
    grads = [
        late_pair(
            pair, slice(pair * PAIR, (pair + 1) * PAIR),
            r_ref, kr_ref, vr_ref, du_ref, au_ref, vu_ref, fv_ref, vec_ref, seg_col_ref,
            seg_row_ref, x_ref, y_ref, u0_ref, s_ref, g_ref, dout_ref, dbg_ref, dfv_out, gvec_ref,
        )
        for pair in range(count)
    ]
    wide = [jnp.concatenate([grads[pair][part] for pair in range(count)], axis=1) for part in range(6)]
    lows = (low0_ref, low1_ref, low2_ref, low3_ref)
    sums = []
    for base in range(pieces):

        @pl.when(step // each == base)
        def arrive(base=base):
            for copy in copies(base, step):
                copy.wait()

    mine_ref = weight_ref.at[step % 2, 0]
    other_ref = weight_ref.at[step % 2, 1]
    extra = jnp.concatenate([gvec_ref[...], early_ref[...]], axis=0)
    up_out[0, BOUNDS[4] : BOUNDS[4] + 16] = extra.astype(up_out.dtype)
    for part in range(3):
        three_ref[0, part] = wide[part]
        sums.append((0, part, mm(wide[part], mine_ref[part], NT)))
        sums.append((1, part, mm(wide[part], other_ref[part], NT)))
    for part in range(4):
        rows = slice(BOUNDS[part], BOUNDS[part + 1])
        up = wide[3 + part] if part < 3 else dgate_ref[...]
        up_out[0, rows] = mm(lows[part][...], up, TN).astype(up_out.dtype)
        sums.append((2 + part, None, mm(up, second_ref[rows], NT)))

    @pl.when(pl.program_id(0) == 0)
    def start():
        for place, part, value in sums:
            ref = places[place]
            if part is None:
                ref[...] = value
            else:
                ref[part] = value

    @pl.when(pl.program_id(0) > 0)
    def add():
        for place, part, value in sums:
            ref = places[place]
            if part is None:
                ref[...] += value
            else:
                ref[part] += value


def late_pair(
    pair, lanes,
    r_ref, kr_ref, vr_ref, du_ref, au_ref, vu_ref, fv_ref, vec_ref, seg_col_ref, seg_row_ref,
    x_ref, y_ref, u0_ref, s_ref, g_ref, dout_ref, dbg_ref, dfv_out, gvec_ref,
):
    vec = vec_ref[:, lanes]
    r = r_ref[:, lanes]
    kr = kr_ref[:, lanes]
    vr = vr_ref[:, lanes]
    fv = fv_ref[:, lanes].astype(F32)
    sig, ld, alpha, vg, mv, scale, unit, mult, sk = prepared(
        kr, vr, du_ref[:, lanes], au_ref[:, lanes], vu_ref[:, lanes], fv, vec
    )
    at, rt, bt, kt, ea, er, eb, lead, tail, through, strict, incl = scaled_parts(
        r, ld, sk, unit, alpha, seg_col_ref[...], seg_row_ref[0:1]
    )
    span = r.shape[0]
    inter = interactions(at, rt, bt, kt, strict, incl)
    state = spread(s_ref[pair])
    grad = spread(g_ref[pair])
    u = u0_ref[:, lanes] + mm(y_ref[:, lanes], state, NT)
    dout = dout_ref[:, lanes]
    dout_half = [part.astype(BF16) for part in halves(dout)]
    first_pass = mm(
        jnp.concatenate(
            [
                jnp.concatenate([inter[0][2], inter[0][3]], axis=1),
                jnp.concatenate([inter[1][2], inter[1][3]], axis=1),
            ],
            axis=0,
        ),
        jnp.concatenate(dout_half, axis=0),
        TN,
    )
    b_tail = bt * tail
    k_tail = kt * tail
    from_grad = mm(jnp.concatenate([b_tail, k_tail], axis=0), grad, NT)
    first_pass = first_pass + from_grad
    d_u = first_pass[:span]
    d_mv = first_pass[span:]
    w = mm(x_ref[pair], jnp.concatenate(halves(d_u), axis=0), TN)
    w_half = [part.astype(BF16) for part in halves(w)]
    d_mv = d_mv + mm(
        jnp.concatenate([inter[0][1], inter[1][1]], axis=0),
        jnp.concatenate(w_half, axis=0),
        TN,
    )
    uv = jnp.concatenate([u, mv], axis=0).astype(BF16)
    bk = jnp.concatenate([bt, kt], axis=0)
    ar = jnp.concatenate([at, rt], axis=0)
    bk_half = halves(bk)
    ar_half = halves(ar)
    d_inter = []
    mask = jnp.concatenate([strict, strict], axis=1)
    mask = jnp.concatenate([mask, mask], axis=0)
    for half in range(2):
        full = mm(jnp.concatenate([w_half[half], dout_half[half]], axis=0), uv, NT)
        d_inter.append(jnp.where(mask, full, 0.0).astype(BF16))
    diag_b = head_sums(dout * u)
    diag_k = head_sums(dout * mv)
    d_ar = mm(jnp.concatenate(d_inter, axis=1), jnp.concatenate(bk_half, axis=0))
    d_bk = mm(jnp.concatenate(d_inter, axis=0), jnp.concatenate(ar_half, axis=0), TN)
    wd = jnp.concatenate([w, dout], axis=0)
    d_in = mm(wd, state)
    d_tail = mm(uv, grad)
    d_at = d_ar[:span] + d_in[:span] * lead
    d_rt = d_ar[span:] + d_in[span:] * lead
    d_bt = d_bk[:span] + d_tail[:span] * tail
    d_kt = d_bk[span:] + d_tail[span:] * tail
    d_before = at * d_at
    d_cum = rt * d_rt - bt * d_bt - kt * d_kt
    at_end = jnp.sum(b_tail * d_tail[:span] + k_tail * d_tail[span:], axis=0, keepdims=True)
    at_end = at_end + through * jnp.sum(s_ref[pair] * g_ref[pair], axis=0, keepdims=True)
    row = lax.broadcasted_iota(jnp.int32, (span, span), 0)
    col = lax.broadcasted_iota(jnp.int32, (span, span), 1)
    triu = jnp.where(row <= col, 1.0, 0.0).astype(BF16)
    d_ld = mm_exact_left(triu, d_cum + d_before) - d_before + at_end
    d_r = d_rt * er + diag_b * (unit * alpha) + diag_k * sk
    d_a = d_at * ea
    d_b = d_bt * eb + diag_b * r
    d_sk = d_kt * eb + diag_k * r
    dbg = dbg_ref[:, lanes]
    extra = head_sums(r * sk * vec[11:12])
    d_extra = head_sums(dbg * mv)
    d_mv = d_mv + dbg * extra
    d_r = d_r + d_extra * sk * vec[11:12]
    d_sk = d_sk + d_extra * r * vec[11:12]
    d_unit = d_b * alpha - d_a
    d_alpha = d_b * unit + d_sk * kr * vec[10:11]
    d_raw = scale * (d_unit - unit * head_sums(d_unit * unit))
    d_kr = d_raw * vec[9:10] + d_sk * mult
    d_du = d_ld * ld * (1.0 - sig)
    d_au = d_alpha * alpha * (1.0 - alpha)
    d_vg = d_mv * (fv - vr)
    d_vu = d_vg * vg * (1.0 - vg)
    dfv_out[:, lanes] = d_mv * vg
    gvec_ref[0:1, lanes] = jnp.sum(d_du, axis=0, keepdims=True)
    gvec_ref[1:2, lanes] = jnp.sum(d_au, axis=0, keepdims=True)
    gvec_ref[2:3, lanes] = jnp.sum(d_vu, axis=0, keepdims=True)
    gvec_ref[3:4, lanes] = jnp.sum(d_raw * kr, axis=0, keepdims=True)
    gvec_ref[4:5, lanes] = jnp.sum(d_sk * kr * (alpha - 1.0), axis=0, keepdims=True)
    gvec_ref[5:6, lanes] = jnp.sum(d_extra * r * sk, axis=0, keepdims=True)
    results = (d_r, d_kr, d_mv * (1.0 - vg), d_du, d_au, d_vu)
    return [value.astype(BF16) for value in results]


def on_core(core_ref, action):
    for core in range(2):
        pl.when(core_ref[0] == core)(lambda core=core: action(core))


def merge_body(core_ref, mine_ref, other_ref, both_ref):
    count = both_ref.shape[0] // 2

    def action(core):
        zero, one = (mine_ref, other_ref) if core == 0 else (other_ref, mine_ref)
        for pair in range(count):
            at = core * count + pair
            moved = mm(jnp.concatenate([zero[0, at], zero[1, at]], axis=0), spread(one[1, at]))
            both_ref[pair] = (one[0, at].astype(F32) + moved[:HEAD]).astype(both_ref.dtype)
            both_ref[count + pair] = moved[HEAD:].astype(both_ref.dtype)

    on_core(core_ref, action)


def state_body(core_ref, chip_ref, swap_ref, other_ref, state_ref):
    count = chip_ref.shape[0]

    def action(core):
        for pair in range(2 * count):
            source = chip_ref if pair // count == core else swap_ref
            value = source[pair % count]
            if core == 0:
                state_ref[pair] = value.astype(F32)
            else:
                state_ref[pair] = other_ref[0, pair].astype(F32) + mm(
                    value, spread(other_ref[1, pair])
                )

    on_core(core_ref, action)


def merge_back_body(core_ref, mine_g_ref, other_g_ref, mine_ref, other_ref, chip_ref):
    count = chip_ref.shape[0]

    def action(core):
        zero, one = (mine_g_ref, other_g_ref) if core == 0 else (other_g_ref, mine_g_ref)
        through = mine_ref if core == 0 else other_ref
        for pair in range(count):
            at = core * count + pair
            chip_ref[pair] = (
                zero[at].astype(F32) + mm(one[at], spread(through[1, at]), NT)
            ).astype(chip_ref.dtype)

    on_core(core_ref, action)


def end_body(core_ref, chip_ref, swap_ref, other_g_ref, other_ref, grad_ref):
    count = chip_ref.shape[0]

    def action(core):
        for pair in range(2 * count):
            source = chip_ref if pair // count == core else swap_ref
            value = source[pair % count]
            if core == 1:
                grad_ref[pair] = value.astype(F32)
            else:
                grad_ref[pair] = other_g_ref[pair].astype(F32) + mm(
                    value, spread(other_ref[1, pair]), NT
                )

    on_core(core_ref, action)


def hop_body(old_ref, o_ref, t_ref, new_ref):
    for pair in range(o_ref.shape[0]):
        new_ref[pair] = (
            o_ref[pair].astype(F32) + mm(old_ref[pair], spread(t_ref[pair]))
        ).astype(new_ref.dtype)


def hop_back_body(old_ref, g_ref, t_ref, new_ref):
    for pair in range(g_ref.shape[0]):
        new_ref[pair] = (
            g_ref[pair].astype(F32) + mm(old_ref[pair], spread(t_ref[pair]), NT)
        ).astype(new_ref.dtype)


def gather_three_body(both_one_ref, both_two_ref, three_ref, state_ref):
    count = three_ref.shape[0]
    for pair in range(count):
        far = both_two_ref[pair].astype(F32) + mm(
            three_ref[pair], spread(both_two_ref[count + pair])
        )
        state_ref[pair] = (
            both_one_ref[pair].astype(F32) + mm(far, spread(both_one_ref[count + pair]))
        ).astype(state_ref.dtype)


def gather_back_body(one_ref, two_ref, three_ref, t_one_ref, t_two_ref, grad_ref):
    for pair in range(three_ref.shape[0]):
        far = two_ref[pair].astype(F32) + mm(three_ref[pair], spread(t_two_ref[pair]), NT)
        grad_ref[pair] = (
            one_ref[pair].astype(F32) + mm(far, spread(t_one_ref[pair]), NT)
        ).astype(grad_ref.dtype)


def cols(span, base=0):
    return pl.BlockSpec((span, BLOCK), lambda step: (0, step + base))


def per_pair(rows, base=0):
    return pl.BlockSpec((BLOCK // PAIR, rows, PAIR), lambda step: (step + base, 0, 0))


def fixed(shape):
    return pl.BlockSpec(shape, lambda step: (0,) * len(shape))


def stacked(shape):
    return pl.BlockSpec(shape + (BLOCK,), lambda step: (0,) * len(shape) + (step,))


def shaped(shape, dtype):
    return jax.ShapeDtypeStruct(shape, dtype)


def forward_call(mixes, weights, lows, second, fv, vec, seg_col, seg_row, base, width, before):
    span, here = fv.shape
    pairs = width // PAIR
    args = [*mixes, *weights, *lows, second, fv, vec, seg_col, seg_row]
    steps = here // BLOCK
    first = base * steps
    in_specs = (
        [fixed(mix.shape) for mix in mixes]
        + [stacked(weights[0].shape[:2])] * 2
        + [fixed(low.shape) for low in lows]
        + [cols(second.shape[0]), cols(span), cols(vec.shape[0])]
        + [fixed(seg_col.shape), fixed(seg_row.shape)]
    )
    aliases = {}
    if before is not None:
        aliases = {len(args) + place: place for place in range(len(before))}
        in_specs = in_specs + [pl.BlockSpec(memory_space=pl.ANY)] * len(before)
        args = args + list(before)
    return pl.pallas_call(
        forward_body,
        grid=(steps,),
        in_specs=in_specs,
        out_specs=[cols(span, first)] * 12
        + [
            per_pair(2 * span, first),
            pl.BlockSpec((2, BLOCK // PAIR, HEAD, PAIR), lambda step: (0, step + first, 0, 0)),
        ],
        out_shape=[shaped((span, width), F32)] * 7
        + [shaped((span, width), BF16)] * 2
        + [shaped((span, width), F32)] * 3
        + [
            shaped((pairs, 2 * span, span), BF16),
            shaped((2, pairs, HEAD, PAIR), BF16),
        ],
        input_output_aliases=aliases,
        name="wkv_forward",
    )(*args)


def finish_call(q, out, bonus, state, gate, vec):
    span, width = out.shape
    return pl.pallas_call(
        finish_body,
        grid=(width // BLOCK,),
        in_specs=[cols(span)] * 3 + [per_pair(HEAD), cols(span), cols(vec.shape[0])],
        out_specs=[cols(span)] * 3,
        out_shape=[
            shaped((span, width), F32), shaped((span, width), F32), shaped((span, width), BF16),
        ],
        name="wkv_finish",
    )(q, out, bonus, state, gate, vec)


def early_call(d_branch, gate, xhat, rstd, bonus, q, vec):
    span, width = xhat.shape
    return pl.pallas_call(
        early_body,
        grid=(width // BLOCK,),
        in_specs=[cols(span)] * 6 + [cols(vec.shape[0])],
        out_specs=[cols(span)] * 3 + [per_pair(HEAD), cols(8)],
        out_shape=[
            shaped((span, width), F32),
            shaped((span, width), F32),
            shaped((span, width), BF16),
            shaped((width // PAIR, HEAD, PAIR), BF16),
            shaped((8, width), F32),
        ],
        name="wkv_early",
    )(d_branch, gate, xhat, rstd, bonus, q, vec)


def late_call(
    raws, fv, vec, seg_col, seg_row, x, y, u0, state, grad, dout, dbg, dgate,
    early, second, lows, weights,
):
    span, width = fv.shape
    steps = width // BLOCK
    half = weights[0][0].shape[1]
    low_shapes = [low.shape for low in lows]
    inner = second.shape[0]
    flat = [array for pair in weights for array in pair]
    return pl.pallas_call(
        late_body,
        grid=(steps,),
        in_specs=[cols(span)] * 7
        + [cols(vec.shape[0]), fixed(seg_col.shape), fixed(seg_row.shape)]
        + [per_pair(2 * span), cols(span), cols(span)]
        + [per_pair(HEAD)] * 2
        + [cols(span)] * 3
        + [cols(8), cols(inner)]
        + [fixed(shape) for shape in low_shapes]
        + [pl.BlockSpec(memory_space=pl.ANY)] * len(flat),
        out_specs=[
            pl.BlockSpec((1, 3, span, BLOCK), lambda step: (step, 0, 0, 0)),
            cols(span),
            pl.BlockSpec((1, inner + 16, BLOCK), lambda step: (step, 0, 0)),
        ]
        + [fixed((3, span, half))] * 2
        + [fixed(shape) for shape in low_shapes],
        out_shape=[
            shaped((steps, 3, span, BLOCK), BF16),
            shaped((span, width), F32),
            shaped((steps, inner + 16, BLOCK), BF16),
            shaped((3, span, half), F32),
            shaped((3, span, half), F32),
        ]
        + [shaped(shape, F32) for shape in low_shapes],
        scratch_shapes=[
            pltpu.VMEM((8, BLOCK), F32),
            pltpu.VMEM((2, 2, 3, half, BLOCK), BF16),
            pltpu.SemaphoreType.DMA((2, 2)),
        ],
        name="wkv_late",
    )(
        *raws, fv, vec, seg_col, seg_row, x, y, u0, state, grad, dout, dbg, dgate,
        early, second, *lows, *flat,
    )


def unpack_body(place_ref, own_ref, rest_ref, mine_ref, other_ref, down_ref, second_ref, rel_ref, abs_ref):
    inner = BOUNDS[4]
    count = mine_ref.shape[0] + 1
    size = own_ref.shape[1]

    def action(core):
        for at in range(count):
            for half in range(2):
                if at == 0:
                    source = (own_ref if half == core else rest_ref)[...]
                else:
                    source = (mine_ref if half == core else other_ref)[at - 1]
                lanes = slice((2 * at + half) * size, (2 * at + half + 1) * size)
                start = ((place_ref[1] ^ at) * 2 + half) * size
                placed = pl.ds(pl.multiple_of(start, size), size)
                rows = source[2 * inner :].astype(F32)
                down_ref[:, placed] = source[:inner]
                second_ref[:, lanes] = source[inner : 2 * inner]
                rel_ref[:, lanes] = rows
                abs_ref[:, placed] = rows

    on_core(place_ref, action)


def unpack_call(place, own, rest, mine, other, width):
    inner = BOUNDS[4]
    rows = own.shape[0] - 2 * inner
    return pl.pallas_call(
        unpack_body,
        in_specs=[pl.BlockSpec(memory_space=pltpu.SMEM)]
        + [pl.BlockSpec(memory_space=pltpu.VMEM)] * 4,
        out_shape=[
            shaped((inner, width), BF16),
            shaped((inner, width), BF16),
            shaped((rows, width), F32),
            shaped((rows, width), F32),
        ],
        name="unpack_small",
    )(place, own, rest, mine, other)


def small_call(body, name, shape, dtype, core, *arrays):
    return pl.pallas_call(
        body,
        in_specs=[pl.BlockSpec(memory_space=pltpu.SMEM)]
        + [pl.BlockSpec(memory_space=pltpu.VMEM)] * len(arrays),
        out_shape=shaped(shape, dtype),
        name=name,
    )(core, *arrays)


def hop_call(body, name, old, add, through):
    return pl.pallas_call(body, out_shape=shaped(add.shape, BF16), name=name)(old, add, through)


def gather_three_call(one, two, three):
    return pl.pallas_call(
        gather_three_body, out_shape=shaped(three.shape, BF16), name="state_gather"
    )(one, two, three)


def gather_back_call(one, two, three, t_one, t_two):
    return pl.pallas_call(
        gather_back_body, out_shape=shaped(three.shape, BF16), name="state_gather_back"
    )(one, two, three, t_one, t_two)


def matmul(left, right):
    return jnp.dot(left, right, preferred_element_type=F32)


def matmul_nt(left, right):
    return lax.dot_general(left, right, NT, preferred_element_type=F32)


def matmul_tn(left, right):
    return lax.dot_general(left, right, TN, preferred_element_type=F32)


def layer_norm(values, gain, bias_row):
    center = values - jnp.mean(values, axis=-1, keepdims=True)
    spread_sq = jnp.mean(center * center, axis=-1, keepdims=True)
    return center * lax.rsqrt(spread_sq + LN_EPS) * gain + bias_row


def blend_rows(current, earlier, keep_row, gain_rows):
    change = earlier * keep_row - current
    return current[None] + change[None] * gain_rows[:, None, :]


def shifted(value, steps):
    count = lax.axis_size("seq")
    initial, last = (max(0, -steps), min(count, count - steps))
    return lax.ppermute(value, "seq", [(place, place + steps) for place in range(initial, last)])


def partner(value, axis, flip):
    count = lax.axis_size(axis)
    return lax.ppermute(value, axis, [(place, place ^ flip) for place in range(count)])


def after(value, *others):
    return lax.optimization_barrier((value,) + others)[0]


def spread_to_group(shard):
    count = lax.axis_size("fsdp")
    return [shard] + [partner(shard, "fsdp", flip) for flip in range(1, count)]


def relay_to_group(shard, axis):
    if lax.axis_size("fsdp") != 4:
        return spread_to_group(shard)
    first = partner(shard, "fsdp", 1)
    second = partner(shard, "fsdp", 2)
    size = shard.shape[axis] // 2
    low = partner(lax.slice_in_dim(first, 0, size, axis=axis), "fsdp", 2)
    high = partner(lax.slice_in_dim(second, size, 2 * size, axis=axis), "fsdp", 1)
    return [shard, first, second, jnp.concatenate([low, high], axis=axis)]


def absolute_order(pieces, me, axis):
    stack = jnp.stack(pieces)
    ordered = [
        lax.dynamic_index_in_dim(stack, me ^ place, 0, False) for place in range(len(pieces))
    ]
    return jnp.concatenate(ordered, axis=axis)


def relative_columns(array, me, count):
    size = array.shape[1] // count
    pieces = [
        lax.dynamic_slice_in_dim(array, (me ^ place) * size, size, 1) for place in range(count)
    ]
    return jnp.concatenate(pieces, axis=1)


def core_halves(array, axis, core):
    size = array.shape[axis] // 2
    mine = lax.dynamic_slice_in_dim(array, core * size, size, axis)
    return (mine, lax.dynamic_slice_in_dim(array, (1 - core) * size, size, axis))


def by_core(core, mine, other):
    return (jnp.where(core == 0, mine, other), jnp.where(core == 0, other, mine))


def join_halves(core, mine, other, axis):
    return jnp.concatenate(by_core(core, mine, other), axis=axis)


def gather_rows(rows):
    return jnp.concatenate(spread_to_group(rows), axis=0)


def scatter_rows(rows):
    count = lax.axis_size("fsdp")
    size = rows.shape[0] // count
    total = rows[:size].astype(F32)
    for flip in range(1, count):
        total = total + partner(rows[flip * size : (flip + 1) * size], "fsdp", flip).astype(F32)
    return total


def column_pieces(array, count):
    size = array.shape[-1] // count
    return [array[..., place * size : (place + 1) * size] for place in range(count)]


def exchange(pieces):
    return [pieces[0]] + [
        partner(pieces[flip], "fsdp", flip) for flip in range(1, len(pieces))
    ]


def as_blocks(pieces):
    if pieces[0].shape[-1] == BLOCK:
        return jnp.stack(pieces)
    joined = jnp.concatenate(pieces, axis=-1)
    split = joined.reshape(joined.shape[:-1] + (-1, BLOCK))
    return jnp.moveaxis(split, -2, 0)


def from_blocks(blocks, count):
    if blocks.shape[0] == count:
        return [blocks[place] for place in range(count)]
    joined = jnp.moveaxis(blocks, 0, -2)
    joined = joined.reshape(joined.shape[:-2] + (-1,))
    return column_pieces(joined, count)


def sum_on_chip(array, core):
    chips = lax.axis_size("seq") // 2
    own, leaving = core_halves(array, 0, core)
    other = partner(leaving, "seq", 1)
    summed = (own.astype(F32) + other.astype(F32)).astype(BF16)
    return summed.reshape(chips, array.shape[0] // (2 * chips), -1)


def sum_over_chips(on_chip, chip):
    total = lax.dynamic_index_in_dim(on_chip, chip, 0, False).astype(F32)
    for flip in range(1, on_chip.shape[0]):
        leaving = lax.dynamic_index_in_dim(on_chip, chip ^ flip, 0, False)
        total = total + partner(leaving, "seq", 2 * flip).astype(F32)
    return total.astype(BF16)


def share_sums(total, core, chip, fence=()):
    chips = lax.axis_size("seq") // 2
    pieces = [total] + [partner(total, "seq", 2 * flip) for flip in range(1, chips)]
    if fence:
        pieces = lax.optimization_barrier(tuple(pieces) + tuple(fence))[:chips]
    mine = absolute_order(pieces, chip, 0)
    return by_core(core, mine, partner(mine, "seq", 1))


def own_pairs(core, array):
    size = array.shape[0] // 2
    return lax.dynamic_slice_in_dim(array, core * size, size, 0)


def all_pairs(core, mine):
    return join_halves(core, mine, partner(mine, "seq", 1), 0)


def body(
    layer_input,
    first_layer_values,
    document_numbers,
    output_cotangent,
    projection_matrices,
    time_output_matrix,
    lowrank_first,
    lowrank_second,
    channel_key_matrix,
    channel_value_matrix,
    vectors,
):
    groups = lax.axis_size("fsdp")
    me = lax.axis_index("fsdp")
    place = lax.axis_index("seq")
    core = place % 2
    chip = place // 2
    chips = lax.axis_size("seq") // 2
    span, width = layer_input.shape[1:]
    here = projection_matrices.shape[2]
    resid_in = layer_input[0].astype(F32)
    cotangent = output_cotangent[0]
    id_plus = document_numbers[0].astype(F32) + 1.0

    edge = jnp.concatenate(
        [resid_in[span - 1 :], jnp.broadcast_to(id_plus[span - 1 :, None], (1, PAIR))], axis=1
    )
    edge = shifted(edge, 1)
    core_flag = core.reshape(1)
    inner = BOUNDS[4]
    vec_count = vectors.shape[0]
    packed = jnp.concatenate(
        [
            lowrank_first.T,
            lowrank_second,
            jnp.concatenate([vectors, jnp.zeros((32 - vec_count, here), BF16)], axis=0),
        ],
        axis=0,
    )
    if here == BLOCK:
        pack_own, pack_rest = core_halves(packed, 1, core)
        pack_mine = jnp.stack(spread_to_group(pack_own)[1:])
        pack_other = partner(pack_mine, "seq", 1)
        down, second, vec_rows, vec = unpack_call(
            jnp.stack([core, me]), pack_own, pack_rest, pack_mine, pack_other, width
        )
    else:
        pack_pieces = spread_to_group(packed)
        relative = jnp.concatenate(pack_pieces, axis=1)
        ordered_pack = absolute_order(pack_pieces, me, 1)
        down = ordered_pack[:inner]
        second = relative[inner : 2 * inner]
        vec_rows = relative[2 * inner :].astype(F32)
        vec = ordered_pack[2 * inner :].astype(F32)
    own_proj, rest_proj = core_halves(projection_matrices, 1, core)
    proj_mine = relay_to_group(own_proj, 1)
    first_rel = relative_columns(first_layer_values[0], me, groups)

    edge_id = edge[0, width]
    earlier_ids = jnp.concatenate([edge[0, width : width + 1], id_plus[:-1]])
    keep_row = (id_plus == earlier_ids).astype(F32)[:, None]
    segment = id_plus - edge_id
    seg_col = jnp.broadcast_to(segment[:, None], (span, PAIR))
    seg_row = jnp.broadcast_to(segment[None], (8, span))

    def mixer(current, earlier, gain_rows):
        return blend_rows(current, earlier, keep_row, gain_rows)

    normed_one, ln_one_back = jax.vjp(layer_norm, resid_in, vec[14], vec[15])
    edge_row = layer_norm(edge[:, :width], vec[14], vec[15])
    earlier_one = jnp.concatenate([edge_row, normed_one[:-1]])
    mixed_rows, mix_back = jax.vjp(mixer, normed_one, earlier_one, vec[0:6])
    mixed = mixed_rows.astype(BF16)
    down_parts = [down[BOUNDS[part] : BOUNDS[part + 1]] for part in range(4)]
    decay_pre = matmul_nt(mixed[1], down_parts[0])
    low_decay = jnp.tanh(decay_pre).astype(BF16)
    low_alpha = matmul_nt(mixed[4], down_parts[1]).astype(BF16)
    low_vmix = matmul_nt(mixed[3], down_parts[2]).astype(BF16)
    gate_pre = matmul_nt(mixed[5], down_parts[3])
    low_gate = jax.nn.sigmoid(gate_pre).astype(BF16)
    lows = (low_decay, low_alpha, low_vmix, low_gate)
    mix_three = jnp.stack([mixed[0], mixed[2], mixed[3]])
    mix_halves = core_halves(mix_three, 2, core)

    if here == BLOCK:
        pieces = proj_mine
    else:
        pieces = [jnp.concatenate(proj_mine, axis=2)]
        rest_proj = partner(pieces[0], "seq", 1)
    chunk = width // len(pieces)
    results = None
    weights = []
    for base, piece in enumerate(pieces):
        lanes = slice(base * chunk, (base + 1) * chunk)
        if base == 0:
            pair = (piece, rest_proj)
        else:
            pair = (piece, partner(piece, "seq", 1))
        weights.append(pair)
        results = forward_call(
            mix_halves, pair, lows, second[:, lanes], first_rel[:, lanes],
            vec_rows[:, lanes], seg_col, seg_row, base, width, results,
        )
        if here == BLOCK and base == 2:
            pieces[3] = after(pieces[3], results[-1])
    raws = results[0:6]
    gate, query, y_part, u_part, out_part, bonus, inverse, both = results[6:]

    out_pieces = spread_to_group(after(core_halves(time_output_matrix, 0, core)[0], both))
    cot_rows = gather_rows(after(cotangent, both))
    mix_pieces = spread_to_group(after(mix_three, both))

    other_both = partner(both, "seq", 1)
    pairs = both.shape[1]
    own = pairs // 2
    chip_both = small_call(
        merge_body, "state_merge", (2 * own,) + both.shape[2:], BF16, core_flag, both, other_both
    )
    chip_offset = chip_both[:own]
    chip_transfer = chip_both[own:]
    if chips == 4:
        arriving = gather_three_call(
            shifted(chip_both, 2), shifted(chip_both, 4), shifted(chip_offset, 6)
        )
        next_transfers = (shifted(chip_transfer, -2), shifted(chip_transfer, -4))
    else:
        arriving = shifted(chip_offset, 2)
        for _ in range(chips - 2):
            arriving = shifted(
                hop_call(hop_body, "state_hop", arriving, chip_offset, chip_transfer), 2
            )
    out_pieces = lax.optimization_barrier(tuple(out_pieces) + (arriving,))[:-1]
    out_mine = jnp.stack(out_pieces)
    out_full = join_halves(core, out_mine, partner(out_mine, "seq", 1), 1).reshape(width, width)
    state = small_call(
        state_body, "state_final", both.shape[1:], F32,
        core_flag, arriving, partner(arriving, "seq", 1), other_both,
    )

    xhat, rstd, branch = finish_call(query, out_part, bonus, state, gate, vec_rows)
    middle = resid_in + matmul(branch, out_full)
    normed_two, ln_two_back = jax.vjp(layer_norm, middle, vec[16], vec[17])
    edge_two = shifted(normed_two[span - 1 :], 1)
    earlier_two = jnp.concatenate([edge_two, normed_two[:-1]])
    cmix_in, cmix_back = jax.vjp(mixer, normed_two, earlier_two, vec[18:19])
    cmix_rows = gather_rows(cmix_in[0].astype(BF16))
    pre_act = matmul(cmix_rows, channel_key_matrix)
    d_hidden = matmul_nt(cot_rows, channel_value_matrix)
    active = jax.nn.relu(pre_act)
    d_pre = (d_hidden * 2.0 * active).astype(BF16)
    d_cmix = scatter_rows(matmul_nt(d_pre, channel_key_matrix).astype(BF16))
    hidden = jnp.square(active).astype(BF16)
    grad_value = matmul_tn(hidden, cot_rows).astype(BF16)
    grad_key = matmul_tn(cmix_rows, d_pre).astype(BF16)
    hidden_out = matmul(hidden, channel_value_matrix).astype(BF16)
    d_cmix, grad_value, grad_key, hidden_out = lax.optimization_barrier(
        (d_cmix, grad_value, grad_key, hidden_out)
    )
    hidden_pieces = exchange([hidden_out[at * span : (at + 1) * span] for at in range(groups)])
    grad_value, grad_key = [
        part.astype(F32) for part in lax.psum((grad_value, grad_key), "seq")
    ]

    d_normed_two, d_earlier_two, d_cmix_gain = cmix_back(d_cmix[None])
    back_two = shifted(d_earlier_two[:1], -1)
    d_middle, d_gain_two, d_bias_two = ln_two_back(
        d_normed_two + jnp.concatenate([d_earlier_two[1:], back_two])
    )
    d_middle = d_middle + cotangent.astype(F32)
    d_middle_b = d_middle.astype(BF16)
    d_branch = matmul_nt(d_middle_b, out_full)
    d_out, d_inner, d_gate, start_grad, vec_early = early_call(
        d_branch, gate, xhat, rstd, bonus, query, vec_rows
    )

    other_start = partner(start_grad, "seq", 1)
    chip_start = small_call(
        merge_back_body, "grad_merge", (own,) + start_grad.shape[1:], BF16,
        core_flag, start_grad, other_start, both, other_both,
    )
    if chips == 4:
        arriving = gather_back_call(
            shifted(chip_start, -2), shifted(chip_start, -4), shifted(chip_start, -6),
            *next_transfers,
        )
    else:
        arriving = shifted(chip_start, -2)
        for _ in range(chips - 2):
            arriving = shifted(
                hop_call(hop_back_body, "grad_hop", arriving, chip_start, chip_transfer), -2
            )
    end_grad = small_call(
        end_body, "grad_final", both.shape[1:], F32,
        core_flag, arriving, partner(arriving, "seq", 1), other_start, other_both,
    )

    three, d_first_rel, ups, mixed_mine, mixed_other, *d_lows = late_call(
        raws, first_rel, vec_rows, seg_col, seg_row,
        inverse, y_part, u_part, state, end_grad, d_out, d_inner, d_gate,
        vec_early, second, lows, weights,
    )

    middle_pieces = spread_to_group(d_middle_b)
    held = lax.optimization_barrier(tuple(mix_pieces) + tuple(middle_pieces) + (three,))
    mix_rows = jnp.concatenate(held[:groups], axis=1)
    middle_rows = jnp.concatenate(held[groups : 2 * groups], axis=0)
    three = held[-1]
    branch_cols = jnp.concatenate(exchange(column_pieces(branch, groups)), axis=0)
    grad_out = matmul_tn(branch_cols, middle_rows)
    grad_out = jnp.concatenate(column_pieces(grad_out, width // here), axis=0)
    head_grads = jnp.concatenate(exchange(from_blocks(three, groups)), axis=1)
    grad_proj = [matmul_tn(mix_rows[part], head_grads[part]) for part in range(3)]
    large = jnp.concatenate(grad_proj + [grad_out], axis=0).astype(BF16)
    large = sum_on_chip(large, core)
    mixed_mine, mixed_other, large = lax.optimization_barrier((mixed_mine, mixed_other, large))
    large = sum_over_chips(large, chip)
    tanh_now = jnp.tanh(decay_pre)
    sigma_now = jax.nn.sigmoid(gate_pre)
    low_grads = (
        (d_lows[0] * (1.0 - tanh_now * tanh_now)).astype(BF16),
        d_lows[1].astype(BF16),
        d_lows[2].astype(BF16),
        (d_lows[3] * sigma_now * (1.0 - sigma_now)).astype(BF16),
    )
    low_mixes = (mixed[1], mixed[4], mixed[3], mixed[5])
    grad_down = jnp.concatenate(
        [matmul_tn(low_grads[part], low_mixes[part]) for part in range(4)], axis=0
    )
    d_wide = join_halves(core, mixed_mine, mixed_other, 2)
    d_mixed = jnp.stack(
        [
            d_wide[0],
            matmul(low_grads[0], down_parts[0]),
            d_wide[1],
            d_wide[2] + matmul(low_grads[2], down_parts[2]),
            matmul(low_grads[1], down_parts[1]),
            matmul(low_grads[3], down_parts[3]),
        ]
    )
    d_normed_one, d_earlier_one, d_mix_gains = mix_back(d_mixed)
    back_one = shifted(d_earlier_one[:1], -1)
    d_resid, d_gain_one, d_bias_one = ln_one_back(
        d_normed_one + jnp.concatenate([d_earlier_one[1:], back_one])
    )
    d_input = d_resid + d_middle

    rows_here = lax.broadcasted_iota(jnp.int32, (16, 1), 0)
    vec_part = jnp.pad(d_mix_gains, ((0, 10), (0, 0)))
    singles = (d_gain_one, d_bias_one, d_gain_two, d_bias_two, d_cmix_gain[0])
    for at, row in enumerate(singles):
        vec_part = vec_part + jnp.where(rows_here == 6 + at, row[None], 0.0)
    ordered = jnp.concatenate([grad_down.astype(BF16), vec_part.astype(BF16)], axis=0)
    up_pieces = from_blocks(ups, groups)
    fill = -2 * (inner + 16) % (32 * chips)
    small = [
        jnp.concatenate(
            [
                up_pieces[at],
                lax.dynamic_slice_in_dim(ordered, (me ^ at) * here, here, 1),
                jnp.zeros((fill, here), BF16),
            ],
            axis=0,
        )
        for at in range(groups)
    ]
    landed = exchange(small)
    total = landed[0].astype(F32)
    for piece in landed[1:]:
        total = total + piece.astype(F32)
    total, large, grad_key, grad_value = lax.optimization_barrier(
        (total.astype(BF16), large, grad_key, grad_value)
    )
    total = sum_over_chips(sum_on_chip(total, core), chip)
    large_low, large_high = share_sums(large, core, chip, (total,))
    total = jnp.concatenate(share_sums(total, core, chip), axis=0).astype(F32)
    hidden_pieces = lax.optimization_barrier(tuple(hidden_pieces) + (large_low,))[:-1]
    block_out = middle
    for piece in hidden_pieces:
        block_out = block_out + piece.astype(F32)
    block_out = block_out.astype(BF16)
    down_at = inner + 16
    mix_at = down_at + inner
    grad_vec = jnp.concatenate(
        [
            total[mix_at : mix_at + 6],
            total[inner : inner + 6],
            total[inner + 8 : inner + 10],
            total[mix_at + 6 : mix_at + 11],
        ],
        axis=0,
    )
    return (
        block_out[None],
        d_input[None],
        relative_columns(d_first_rel, me, groups)[None],
        jnp.stack([large_low[:width], large_low[width:], large_high[:width]]).astype(F32),
        jnp.concatenate(
            [large_high[width + at : width + at + here] for at in range(0, width, here)], axis=1
        ).astype(F32),
        total[down_at:mix_at].T,
        total[:inner],
        grad_key,
        grad_value,
        grad_vec,
    )


def solution(mesh):
    in_specs = (
        P("fsdp", "seq", None),
        P("fsdp", "seq", None),
        P("fsdp", "seq"),
        P("fsdp", "seq", None),
        P(None, None, "fsdp"),
        P("fsdp", None),
        P("fsdp", None),
        P(None, "fsdp"),
        P(None, "fsdp"),
        P("fsdp", None),
        P(None, "fsdp"),
    )
    out_specs = (
        P("fsdp", "seq", None),
        P("fsdp", "seq", None),
        P("fsdp", "seq", None),
        P(None, None, "fsdp"),
        P("fsdp", None),
        P("fsdp", None),
        P(None, "fsdp"),
        P(None, "fsdp"),
        P("fsdp", None),
        P(None, "fsdp"),
    )
    return jax.shard_map(body, mesh=mesh, in_specs=in_specs, out_specs=out_specs, check_vma=False)
```

```python
import jax
import jax.numpy as jnp
from jax import lax
from jax.experimental import pallas as pl
from jax.experimental.pallas import tpu as pltpu
from jax.sharding import PartitionSpec as P

F32 = jnp.float32
BF16 = jnp.bfloat16
HEAD = 64
PAIR = 128
BLOCK = 256
BOUNDS = (0, 64, 128, 160, 288)
LN_EPS = 1e-05
GROUP_EPS = 0.00064
UNIT_EPS = 1e-06
NN = (((1,), (0,)), ((), ()))
NT = (((1,), (1,)), ((), ()))
TN = (((0,), (0,)), ((), ()))


def mm(left, right, dims=NN):
    return lax.dot_general(
        left.astype(BF16), right.astype(BF16), dims, preferred_element_type=F32
    )


def mm_exact_left(left, right, dims=NN):
    high = right.astype(BF16)
    low = (right - high.astype(F32)).astype(BF16)
    return lax.dot_general(left, high, dims, preferred_element_type=F32) + lax.dot_general(
        left, low, dims, preferred_element_type=F32
    )


def mm_exact_right(left, right):
    high = left.astype(BF16)
    low = (left - high.astype(F32)).astype(BF16)
    return lax.dot_general(high, right, NN, preferred_element_type=F32) + lax.dot_general(
        low, right, NN, preferred_element_type=F32
    )


def lane_halves(shape):
    lane = lax.broadcasted_iota(jnp.int32, shape, 1)
    return lane < HEAD


def halves(array):
    first = lane_halves(array.shape)
    zero = jnp.zeros_like(array)
    return (jnp.where(first, array, zero), jnp.where(first, zero, array))


def head_sums(array):
    row = lax.broadcasted_iota(jnp.int32, (PAIR, PAIR), 0)
    col = lax.broadcasted_iota(jnp.int32, (PAIR, PAIR), 1)
    ones = jnp.where((row < HEAD) == (col < HEAD), 1.0, 0.0).astype(BF16)
    return mm_exact_right(array, ones)


def compact(block):
    return jnp.where(lane_halves((HEAD, PAIR)), block[:HEAD], block[HEAD:])


def spread(pair):
    return jnp.concatenate(halves(pair), axis=0)


def prepared(kr, vr, du, au, vu, fv, vec):
    decay_in = vec[6:7] + du
    sig = jax.nn.sigmoid(decay_in)
    ld = sig * (-0.6065306597126334)
    alpha = jax.nn.sigmoid(vec[7:8] + au)
    vg = jax.nn.sigmoid(vec[8:9] + vu)
    mv = vr + (fv - vr) * vg
    raw_unit = kr * vec[9:10]
    scale = lax.rsqrt(head_sums(raw_unit * raw_unit) + UNIT_EPS)
    unit = raw_unit * scale
    mult = 1.0 + (alpha - 1.0) * vec[10:11]
    sk = kr * mult
    return (sig, ld, alpha, vg, mv, scale, unit, mult, sk)


def scaled_parts(r, ld, sk, unit, alpha, seg_col, seg_row):
    span = r.shape[0]
    row = lax.broadcasted_iota(jnp.int32, (span, span), 0)
    col = lax.broadcasted_iota(jnp.int32, (span, span), 1)
    tril = jnp.where(row >= col, 1.0, 0.0).astype(BF16)
    cum = mm_exact_left(tril, ld)
    mid = cum[span // 2 - 1 : span // 2]
    end = cum[span - 1 : span]
    ea = jnp.exp(cum - ld - mid)
    er = jnp.exp(cum - mid)
    eb = jnp.exp(mid - cum)
    at = -unit * ea
    rt = r * er
    bt = unit * alpha * eb
    kt = sk * eb
    fresh = jnp.where(seg_col == 0.0, 1.0, 0.0)
    lead = jnp.exp(mid) * fresh
    tail = jnp.exp(end - mid) * jnp.where(seg_col == seg_col[span - 1 : span], 1.0, 0.0)
    through = jnp.exp(end) * fresh[span - 1 : span]
    same = seg_col[:, :span] == seg_row
    strict = same & (row > col)
    incl = same & (row >= col)
    return (at, rt, bt, kt, ea, er, eb, lead, tail, through, strict, incl)


def split_terms(array):
    high = array.astype(BF16)
    return (high, (array - high.astype(F32)).astype(BF16))


def interactions(at, rt, bt, kt, strict, incl):
    span = at.shape[0]
    left_high, left_low = split_terms(jnp.concatenate([at, rt], axis=0))
    right_high, right_low = split_terms(jnp.concatenate([bt, kt], axis=0))
    left_high = halves(left_high)
    left_low = halves(left_low)
    right = jnp.concatenate([right_high, right_high, right_low], axis=1)
    result = []
    for half in range(2):
        left = jnp.concatenate([left_high[half], left_low[half], left_high[half]], axis=1)
        full = mm(left, right, NT)
        result.append(
            (
                jnp.where(strict, full[:span, :span], 0.0),
                jnp.where(strict, full[:span, span:], 0.0),
                jnp.where(incl, full[span:, :span], 0.0),
                jnp.where(incl, full[span:, span:], 0.0),
            )
        )
    return result


def unit_inverses(lowers):
    span = lowers[0].shape[0]
    row = lax.broadcasted_iota(jnp.int32, (span, span), 0)
    col = lax.broadcasted_iota(jnp.int32, (span, span), 1)
    differ = row ^ col
    eye = jnp.where(row == col, 1.0, 0.0)
    solved = [eye + jnp.where(differ == 1, lower, 0.0) for lower in lowers]
    size = 2
    while size < span:
        between = (differ >= size) & (differ < 2 * size)
        parts = [jnp.where(between, lower, 0.0) for lower in lowers]
        inner = [mm(part, done) for part, done in zip(parts, solved)]
        solved = [done + mm(done, part) for done, part in zip(solved, inner)]
        size *= 2
    return solved


def forward_body(
    mine_mix_ref, other_mix_ref, mine_ref, other_ref,
    low0_ref, low1_ref, low2_ref, low3_ref, second_ref,
    fv_ref, vec_ref, seg_col_ref, seg_row_ref, *refs
):
    outs = refs[len(refs) - 14 :]
    raw_refs = outs[0:6]
    gate_ref, q_ref, y_ref, u0_ref, out_ref, bonus_ref, x_ref, both_ref = outs[6:]
    for part in range(3):
        raw_refs[part][...] = mm(mine_mix_ref[part], mine_ref[part]) + mm(
            other_mix_ref[part], other_ref[part]
        )
    lows = (low0_ref, low1_ref, low2_ref, low3_ref)
    for part in range(4):
        target = raw_refs[3 + part] if part < 3 else gate_ref
        target[...] = mm(lows[part][...], second_ref[BOUNDS[part] : BOUNDS[part + 1]])
    count = fv_ref.shape[1] // PAIR
    early = []
    for pair in range(count):
        lanes = slice(pair * PAIR, (pair + 1) * PAIR)
        vec = vec_ref[:, lanes]
        r, kr, vr, du, au, vu = [ref[:, lanes] for ref in raw_refs]
        sig, ld, alpha, vg, mv, scale, unit, mult, sk = prepared(
            kr, vr, du, au, vu, fv_ref[:, lanes].astype(F32), vec
        )
        at, rt, bt, kt, ea, er, eb, lead, tail, through, strict, incl = scaled_parts(
            r, ld, sk, unit, alpha, seg_col_ref[...], seg_row_ref[0:1]
        )
        inter = interactions(at, rt, bt, kt, strict, incl)
        bonus_ref[:, lanes] = head_sums(r * sk * vec[11:12]) * mv
        early.append((mv, at * lead, rt * lead, bt * tail, kt * tail, through, inter))
    found = unit_inverses([item[6][half][0] for item in early for half in range(2)])
    for pair in range(count):
        lanes = slice(pair * PAIR, (pair + 1) * PAIR)
        mv, a_in, r_in, b_tail, k_tail, through, inter = early[pair]
        inverse = found[2 * pair : 2 * pair + 2]
        v_half = [part.astype(BF16) for part in halves(mv)]
        av = mm(
            jnp.concatenate([inter[0][1], inter[1][1]], axis=1),
            jnp.concatenate(v_half, axis=0),
        )
        right = jnp.concatenate([av, a_in], axis=1)
        first = lax.broadcasted_iota(jnp.int32, right.shape, 1) % PAIR < HEAD
        solved = mm(
            jnp.concatenate(inverse, axis=1),
            jnp.concatenate([jnp.where(first, right, 0.0), jnp.where(first, 0.0, right)], axis=0),
        )
        u0 = solved[:, :PAIR]
        y = solved[:, PAIR:]
        uy = solved.astype(BF16)
        zero = jnp.zeros_like(uy)
        zero_half = jnp.zeros_like(v_half[0])
        joined = mm(
            jnp.concatenate([inter[0][2], inter[1][2], inter[0][3], inter[1][3]], axis=1),
            jnp.concatenate(
                [
                    jnp.where(first, uy, zero),
                    jnp.where(first, zero, uy),
                    jnp.concatenate([v_half[0], zero_half], axis=1),
                    jnp.concatenate([v_half[1], zero_half], axis=1),
                ],
                axis=0,
            ),
        )
        q_ref[:, lanes] = (r_in + joined[:, PAIR:]).astype(q_ref.dtype)
        out_ref[:, lanes] = joined[:, :PAIR]
        y_ref[:, lanes] = y.astype(y_ref.dtype)
        u0_ref[:, lanes] = u0
        diag_row = lax.broadcasted_iota(jnp.int32, (PAIR, PAIR), 0)
        diag_col = lax.broadcasted_iota(jnp.int32, (PAIR, PAIR), 1)
        transfer = mm(y, b_tail, TN) + jnp.where(diag_row == diag_col, through, 0.0)
        offset = mm(
            jnp.concatenate([u0, mv], axis=0), jnp.concatenate([b_tail, k_tail], axis=0), TN
        )
        both_ref[0, pair] = compact(offset).astype(both_ref.dtype)
        both_ref[1, pair] = compact(transfer).astype(both_ref.dtype)
        x_ref[pair] = jnp.concatenate(inverse, axis=0).astype(x_ref.dtype)


def finish_body(q_ref, out_ref, bonus_ref, s_ref, gate_ref, vec_ref, xhat_ref, rstd_ref, branch_ref):
    for pair in range(out_ref.shape[1] // PAIR):
        lanes = slice(pair * PAIR, (pair + 1) * PAIR)
        vec = vec_ref[:, lanes]
        out = out_ref[:, lanes] + mm(q_ref[:, lanes], spread(s_ref[pair]), NT)
        center = out - head_sums(out) * (1.0 / HEAD)
        rstd = lax.rsqrt(head_sums(center * center) * (1.0 / HEAD) + GROUP_EPS)
        xhat = center * rstd
        xhat_ref[:, lanes] = xhat
        rstd_ref[:, lanes] = rstd
        branch_ref[:, lanes] = (
            (xhat * vec[12:13] + vec[13:14] + bonus_ref[:, lanes]) * gate_ref[:, lanes]
        ).astype(branch_ref.dtype)


def early_body(
    db_ref, gate_ref, xhat_ref, rstd_ref, bonus_ref, q_ref, vec_ref,
    dout_ref, dbg_ref, dgate_ref, gs_ref, gvec_ref,
):
    gvec_ref[...] = jnp.zeros_like(gvec_ref)
    for pair in range(db_ref.shape[1] // PAIR):
        lanes = slice(pair * PAIR, (pair + 1) * PAIR)
        vec = vec_ref[:, lanes]
        d_branch = db_ref[:, lanes]
        xhat = xhat_ref[:, lanes]
        inner = xhat * vec[12:13] + vec[13:14] + bonus_ref[:, lanes]
        dgate_ref[:, lanes] = (d_branch * inner).astype(dgate_ref.dtype)
        dbg = d_branch * gate_ref[:, lanes]
        dbg_ref[:, lanes] = dbg
        dn = dbg * vec[12:13]
        dout = rstd_ref[:, lanes] * (
            dn - head_sums(dn) * (1.0 / HEAD) - xhat * (head_sums(dn * xhat) * (1.0 / HEAD))
        )
        dout_ref[:, lanes] = dout
        gs_ref[pair] = compact(mm(dout, q_ref[:, lanes], TN)).astype(gs_ref.dtype)
        gvec_ref[0:1, lanes] = jnp.sum(dbg * xhat, axis=0, keepdims=True)
        gvec_ref[1:2, lanes] = jnp.sum(dbg, axis=0, keepdims=True)


def late_body(
    r_ref, kr_ref, vr_ref, du_ref, au_ref, vu_ref, fv_ref, vec_ref, seg_col_ref, seg_row_ref,
    x_ref, y_ref, u0_ref, s_ref, g_ref, dout_ref, dbg_ref, dgate_ref,
    early_ref, second_ref, low0_ref, low1_ref, low2_ref, low3_ref, *refs
):
    gvec_ref, weight_ref, sem = refs[len(refs) - 3 :]
    outs = refs[len(refs) - 12 : len(refs) - 3]
    sources = refs[: len(refs) - 12]
    pieces = len(sources) // 2
    three_ref, dfv_out, up_out = outs[:3]
    mine_out, other_out, l0_out, l1_out, l2_out, l3_out = outs[3:]
    step = pl.program_id(0)
    each = sources[0].shape[2] // BLOCK

    def copies(base, at):
        found = []
        for side in range(2):
            source = sources[2 * base + side]
            if each > 1:
                source = source.at[:, :, pl.ds(pl.multiple_of(at * BLOCK, BLOCK), BLOCK)]
            found.append(
                pltpu.make_async_copy(source, weight_ref.at[at % 2, side], sem.at[at % 2, side])
            )
        return found

    @pl.when(step == 0)
    def fetch_first():
        for copy in copies(0, step):
            copy.start()

    for base in range(pieces):

        @pl.when(((step + 1) // each == base) & (step + 1 < pl.num_programs(0)))
        def fetch(base=base):
            for copy in copies(base, step + 1):
                copy.start()

    places = {0: mine_out, 1: other_out, 2: l0_out, 3: l1_out, 4: l2_out, 5: l3_out}
    gvec_ref[...] = jnp.zeros_like(gvec_ref)
    count = fv_ref.shape[1] // PAIR
    grads = [
        late_pair(
            pair, slice(pair * PAIR, (pair + 1) * PAIR),
            r_ref, kr_ref, vr_ref, du_ref, au_ref, vu_ref, fv_ref, vec_ref, seg_col_ref,
            seg_row_ref, x_ref, y_ref, u0_ref, s_ref, g_ref, dout_ref, dbg_ref, dfv_out, gvec_ref,
        )
        for pair in range(count)
    ]
    wide = [jnp.concatenate([grads[pair][part] for pair in range(count)], axis=1) for part in range(6)]
    lows = (low0_ref, low1_ref, low2_ref, low3_ref)
    sums = []
    for base in range(pieces):

        @pl.when(step // each == base)
        def arrive(base=base):
            for copy in copies(base, step):
                copy.wait()

    mine_ref = weight_ref.at[step % 2, 0]
    other_ref = weight_ref.at[step % 2, 1]
    extra = jnp.concatenate([gvec_ref[...], early_ref[...]], axis=0)
    up_out[0, BOUNDS[4] : BOUNDS[4] + 16] = extra.astype(up_out.dtype)
    for part in range(3):
        three_ref[0, part] = wide[part]
        sums.append((0, part, mm(wide[part], mine_ref[part], NT)))
        sums.append((1, part, mm(wide[part], other_ref[part], NT)))
    for part in range(4):
        rows = slice(BOUNDS[part], BOUNDS[part + 1])
        up = wide[3 + part] if part < 3 else dgate_ref[...]
        up_out[0, rows] = mm(lows[part][...], up, TN).astype(up_out.dtype)
        sums.append((2 + part, None, mm(up, second_ref[rows], NT)))

    @pl.when(pl.program_id(0) == 0)
    def start():
        for place, part, value in sums:
            ref = places[place]
            if part is None:
                ref[...] = value
            else:
                ref[part] = value

    @pl.when(pl.program_id(0) > 0)
    def add():
        for place, part, value in sums:
            ref = places[place]
            if part is None:
                ref[...] += value
            else:
                ref[part] += value


def late_pair(
    pair, lanes,
    r_ref, kr_ref, vr_ref, du_ref, au_ref, vu_ref, fv_ref, vec_ref, seg_col_ref, seg_row_ref,
    x_ref, y_ref, u0_ref, s_ref, g_ref, dout_ref, dbg_ref, dfv_out, gvec_ref,
):
    vec = vec_ref[:, lanes]
    r = r_ref[:, lanes]
    kr = kr_ref[:, lanes]
    vr = vr_ref[:, lanes]
    fv = fv_ref[:, lanes].astype(F32)
    sig, ld, alpha, vg, mv, scale, unit, mult, sk = prepared(
        kr, vr, du_ref[:, lanes], au_ref[:, lanes], vu_ref[:, lanes], fv, vec
    )
    at, rt, bt, kt, ea, er, eb, lead, tail, through, strict, incl = scaled_parts(
        r, ld, sk, unit, alpha, seg_col_ref[...], seg_row_ref[0:1]
    )
    span = r.shape[0]
    inter = interactions(at, rt, bt, kt, strict, incl)
    state = spread(s_ref[pair])
    grad = spread(g_ref[pair])
    u = u0_ref[:, lanes] + mm(y_ref[:, lanes], state, NT)
    dout = dout_ref[:, lanes]
    dout_half = [part.astype(BF16) for part in halves(dout)]
    first_pass = mm(
        jnp.concatenate(
            [
                jnp.concatenate([inter[0][2], inter[0][3]], axis=1),
                jnp.concatenate([inter[1][2], inter[1][3]], axis=1),
            ],
            axis=0,
        ),
        jnp.concatenate(dout_half, axis=0),
        TN,
    )
    b_tail = bt * tail
    k_tail = kt * tail
    from_grad = mm(jnp.concatenate([b_tail, k_tail], axis=0), grad, NT)
    first_pass = first_pass + from_grad
    d_u = first_pass[:span]
    d_mv = first_pass[span:]
    w = mm(x_ref[pair], jnp.concatenate(halves(d_u), axis=0), TN)
    w_half = [part.astype(BF16) for part in halves(w)]
    d_mv = d_mv + mm(
        jnp.concatenate([inter[0][1], inter[1][1]], axis=0),
        jnp.concatenate(w_half, axis=0),
        TN,
    )
    uv = jnp.concatenate([u, mv], axis=0).astype(BF16)
    bk = jnp.concatenate([bt, kt], axis=0)
    ar = jnp.concatenate([at, rt], axis=0)
    bk_half = halves(bk)
    ar_half = halves(ar)
    d_inter = []
    mask = jnp.concatenate([strict, strict], axis=1)
    mask = jnp.concatenate([mask, mask], axis=0)
    for half in range(2):
        full = mm(jnp.concatenate([w_half[half], dout_half[half]], axis=0), uv, NT)
        d_inter.append(jnp.where(mask, full, 0.0).astype(BF16))
    diag_b = head_sums(dout * u)
    diag_k = head_sums(dout * mv)
    d_ar = mm(jnp.concatenate(d_inter, axis=1), jnp.concatenate(bk_half, axis=0))
    d_bk = mm(jnp.concatenate(d_inter, axis=0), jnp.concatenate(ar_half, axis=0), TN)
    wd = jnp.concatenate([w, dout], axis=0)
    d_in = mm(wd, state)
    d_tail = mm(uv, grad)
    d_at = d_ar[:span] + d_in[:span] * lead
    d_rt = d_ar[span:] + d_in[span:] * lead
    d_bt = d_bk[:span] + d_tail[:span] * tail
    d_kt = d_bk[span:] + d_tail[span:] * tail
    d_before = at * d_at
    d_cum = rt * d_rt - bt * d_bt - kt * d_kt
    at_end = jnp.sum(b_tail * d_tail[:span] + k_tail * d_tail[span:], axis=0, keepdims=True)
    at_end = at_end + through * jnp.sum(s_ref[pair] * g_ref[pair], axis=0, keepdims=True)
    row = lax.broadcasted_iota(jnp.int32, (span, span), 0)
    col = lax.broadcasted_iota(jnp.int32, (span, span), 1)
    triu = jnp.where(row <= col, 1.0, 0.0).astype(BF16)
    d_ld = mm_exact_left(triu, d_cum + d_before) - d_before + at_end
    d_r = d_rt * er + diag_b * (unit * alpha) + diag_k * sk
    d_a = d_at * ea
    d_b = d_bt * eb + diag_b * r
    d_sk = d_kt * eb + diag_k * r
    dbg = dbg_ref[:, lanes]
    extra = head_sums(r * sk * vec[11:12])
    d_extra = head_sums(dbg * mv)
    d_mv = d_mv + dbg * extra
    d_r = d_r + d_extra * sk * vec[11:12]
    d_sk = d_sk + d_extra * r * vec[11:12]
    d_unit = d_b * alpha - d_a
    d_alpha = d_b * unit + d_sk * kr * vec[10:11]
    d_raw = scale * (d_unit - unit * head_sums(d_unit * unit))
    d_kr = d_raw * vec[9:10] + d_sk * mult
    d_du = d_ld * ld * (1.0 - sig)
    d_au = d_alpha * alpha * (1.0 - alpha)
    d_vg = d_mv * (fv - vr)
    d_vu = d_vg * vg * (1.0 - vg)
    dfv_out[:, lanes] = d_mv * vg
    gvec_ref[0:1, lanes] = jnp.sum(d_du, axis=0, keepdims=True)
    gvec_ref[1:2, lanes] = jnp.sum(d_au, axis=0, keepdims=True)
    gvec_ref[2:3, lanes] = jnp.sum(d_vu, axis=0, keepdims=True)
    gvec_ref[3:4, lanes] = jnp.sum(d_raw * kr, axis=0, keepdims=True)
    gvec_ref[4:5, lanes] = jnp.sum(d_sk * kr * (alpha - 1.0), axis=0, keepdims=True)
    gvec_ref[5:6, lanes] = jnp.sum(d_extra * r * sk, axis=0, keepdims=True)
    results = (d_r, d_kr, d_mv * (1.0 - vg), d_du, d_au, d_vu)
    return [value.astype(BF16) for value in results]


def on_core(core_ref, action):
    for core in range(2):
        pl.when(core_ref[0] == core)(lambda core=core: action(core))


def merge_body(core_ref, mine_ref, other_ref, both_ref):
    count = both_ref.shape[0] // 2

    def action(core):
        zero, one = (mine_ref, other_ref) if core == 0 else (other_ref, mine_ref)
        for pair in range(count):
            at = core * count + pair
            moved = mm(jnp.concatenate([zero[0, at], zero[1, at]], axis=0), spread(one[1, at]))
            both_ref[pair] = (one[0, at].astype(F32) + moved[:HEAD]).astype(both_ref.dtype)
            both_ref[count + pair] = moved[HEAD:].astype(both_ref.dtype)

    on_core(core_ref, action)


def state_body(core_ref, chip_ref, swap_ref, other_ref, state_ref):
    count = chip_ref.shape[0]

    def action(core):
        for pair in range(2 * count):
            source = chip_ref if pair // count == core else swap_ref
            value = source[pair % count]
            if core == 0:
                state_ref[pair] = value.astype(F32)
            else:
                state_ref[pair] = other_ref[0, pair].astype(F32) + mm(
                    value, spread(other_ref[1, pair])
                )

    on_core(core_ref, action)


def merge_back_body(core_ref, mine_g_ref, other_g_ref, mine_ref, other_ref, chip_ref):
    count = chip_ref.shape[0]

    def action(core):
        zero, one = (mine_g_ref, other_g_ref) if core == 0 else (other_g_ref, mine_g_ref)
        through = mine_ref if core == 0 else other_ref
        for pair in range(count):
            at = core * count + pair
            chip_ref[pair] = (
                zero[at].astype(F32) + mm(one[at], spread(through[1, at]), NT)
            ).astype(chip_ref.dtype)

    on_core(core_ref, action)


def end_body(core_ref, chip_ref, swap_ref, other_g_ref, other_ref, grad_ref):
    count = chip_ref.shape[0]

    def action(core):
        for pair in range(2 * count):
            source = chip_ref if pair // count == core else swap_ref
            value = source[pair % count]
            if core == 1:
                grad_ref[pair] = value.astype(F32)
            else:
                grad_ref[pair] = other_g_ref[pair].astype(F32) + mm(
                    value, spread(other_ref[1, pair]), NT
                )

    on_core(core_ref, action)


def hop_body(old_ref, o_ref, t_ref, new_ref):
    for pair in range(o_ref.shape[0]):
        new_ref[pair] = (
            o_ref[pair].astype(F32) + mm(old_ref[pair], spread(t_ref[pair]))
        ).astype(new_ref.dtype)


def hop_back_body(old_ref, g_ref, t_ref, new_ref):
    for pair in range(g_ref.shape[0]):
        new_ref[pair] = (
            g_ref[pair].astype(F32) + mm(old_ref[pair], spread(t_ref[pair]), NT)
        ).astype(new_ref.dtype)


def gather_three_body(both_one_ref, both_two_ref, three_ref, state_ref):
    count = three_ref.shape[0]
    for pair in range(count):
        far = both_two_ref[pair].astype(F32) + mm(
            three_ref[pair], spread(both_two_ref[count + pair])
        )
        state_ref[pair] = (
            both_one_ref[pair].astype(F32) + mm(far, spread(both_one_ref[count + pair]))
        ).astype(state_ref.dtype)


def gather_back_body(one_ref, two_ref, three_ref, t_one_ref, t_two_ref, grad_ref):
    for pair in range(three_ref.shape[0]):
        far = two_ref[pair].astype(F32) + mm(three_ref[pair], spread(t_two_ref[pair]), NT)
        grad_ref[pair] = (
            one_ref[pair].astype(F32) + mm(far, spread(t_one_ref[pair]), NT)
        ).astype(grad_ref.dtype)


def cols(span, base=0):
    return pl.BlockSpec((span, BLOCK), lambda step: (0, step + base))


def per_pair(rows, base=0):
    return pl.BlockSpec((BLOCK // PAIR, rows, PAIR), lambda step: (step + base, 0, 0))


def fixed(shape):
    return pl.BlockSpec(shape, lambda step: (0,) * len(shape))


def stacked(shape):
    return pl.BlockSpec(shape + (BLOCK,), lambda step: (0,) * len(shape) + (step,))


def shaped(shape, dtype):
    return jax.ShapeDtypeStruct(shape, dtype)


def forward_call(mixes, weights, lows, second, fv, vec, seg_col, seg_row, base, width, before):
    span, here = fv.shape
    pairs = width // PAIR
    args = [*mixes, *weights, *lows, second, fv, vec, seg_col, seg_row]
    steps = here // BLOCK
    first = base * steps
    in_specs = (
        [fixed(mix.shape) for mix in mixes]
        + [stacked(weights[0].shape[:2])] * 2
        + [fixed(low.shape) for low in lows]
        + [cols(second.shape[0]), cols(span), cols(vec.shape[0])]
        + [fixed(seg_col.shape), fixed(seg_row.shape)]
    )
    aliases = {}
    if before is not None:
        aliases = {len(args) + place: place for place in range(len(before))}
        in_specs = in_specs + [pl.BlockSpec(memory_space=pl.ANY)] * len(before)
        args = args + list(before)
    return pl.pallas_call(
        forward_body,
        grid=(steps,),
        in_specs=in_specs,
        out_specs=[cols(span, first)] * 12
        + [
            per_pair(2 * span, first),
            pl.BlockSpec((2, BLOCK // PAIR, HEAD, PAIR), lambda step: (0, step + first, 0, 0)),
        ],
        out_shape=[shaped((span, width), F32)] * 7
        + [shaped((span, width), BF16)] * 2
        + [shaped((span, width), F32)] * 3
        + [
            shaped((pairs, 2 * span, span), BF16),
            shaped((2, pairs, HEAD, PAIR), BF16),
        ],
        input_output_aliases=aliases,
        name="wkv_forward",
    )(*args)


def finish_call(q, out, bonus, state, gate, vec):
    span, width = out.shape
    return pl.pallas_call(
        finish_body,
        grid=(width // BLOCK,),
        in_specs=[cols(span)] * 3 + [per_pair(HEAD), cols(span), cols(vec.shape[0])],
        out_specs=[cols(span)] * 3,
        out_shape=[
            shaped((span, width), F32), shaped((span, width), F32), shaped((span, width), BF16),
        ],
        name="wkv_finish",
    )(q, out, bonus, state, gate, vec)


def early_call(d_branch, gate, xhat, rstd, bonus, q, vec):
    span, width = xhat.shape
    return pl.pallas_call(
        early_body,
        grid=(width // BLOCK,),
        in_specs=[cols(span)] * 6 + [cols(vec.shape[0])],
        out_specs=[cols(span)] * 3 + [per_pair(HEAD), cols(8)],
        out_shape=[
            shaped((span, width), F32),
            shaped((span, width), F32),
            shaped((span, width), BF16),
            shaped((width // PAIR, HEAD, PAIR), BF16),
            shaped((8, width), F32),
        ],
        name="wkv_early",
    )(d_branch, gate, xhat, rstd, bonus, q, vec)


def late_call(
    raws, fv, vec, seg_col, seg_row, x, y, u0, state, grad, dout, dbg, dgate,
    early, second, lows, weights,
):
    span, width = fv.shape
    steps = width // BLOCK
    half = weights[0][0].shape[1]
    low_shapes = [low.shape for low in lows]
    inner = second.shape[0]
    flat = [array for pair in weights for array in pair]
    return pl.pallas_call(
        late_body,
        grid=(steps,),
        in_specs=[cols(span)] * 7
        + [cols(vec.shape[0]), fixed(seg_col.shape), fixed(seg_row.shape)]
        + [per_pair(2 * span), cols(span), cols(span)]
        + [per_pair(HEAD)] * 2
        + [cols(span)] * 3
        + [cols(8), cols(inner)]
        + [fixed(shape) for shape in low_shapes]
        + [pl.BlockSpec(memory_space=pl.ANY)] * len(flat),
        out_specs=[
            pl.BlockSpec((1, 3, span, BLOCK), lambda step: (step, 0, 0, 0)),
            cols(span),
            pl.BlockSpec((1, inner + 16, BLOCK), lambda step: (step, 0, 0)),
        ]
        + [fixed((3, span, half))] * 2
        + [fixed(shape) for shape in low_shapes],
        out_shape=[
            shaped((steps, 3, span, BLOCK), BF16),
            shaped((span, width), F32),
            shaped((steps, inner + 16, BLOCK), BF16),
            shaped((3, span, half), F32),
            shaped((3, span, half), F32),
        ]
        + [shaped(shape, F32) for shape in low_shapes],
        scratch_shapes=[
            pltpu.VMEM((8, BLOCK), F32),
            pltpu.VMEM((2, 2, 3, half, BLOCK), BF16),
            pltpu.SemaphoreType.DMA((2, 2)),
        ],
        name="wkv_late",
    )(
        *raws, fv, vec, seg_col, seg_row, x, y, u0, state, grad, dout, dbg, dgate,
        early, second, *lows, *flat,
    )


def unpack_body(place_ref, own_ref, rest_ref, mine_ref, other_ref, down_ref, second_ref, rel_ref, abs_ref):
    inner = BOUNDS[4]
    count = mine_ref.shape[0] + 1
    size = own_ref.shape[1]

    def action(core):
        for at in range(count):
            for half in range(2):
                if at == 0:
                    source = (own_ref if half == core else rest_ref)[...]
                else:
                    source = (mine_ref if half == core else other_ref)[at - 1]
                lanes = slice((2 * at + half) * size, (2 * at + half + 1) * size)
                start = ((place_ref[1] ^ at) * 2 + half) * size
                placed = pl.ds(pl.multiple_of(start, size), size)
                rows = source[2 * inner :].astype(F32)
                down_ref[:, placed] = source[:inner]
                second_ref[:, lanes] = source[inner : 2 * inner]
                rel_ref[:, lanes] = rows
                abs_ref[:, placed] = rows

    on_core(place_ref, action)


def unpack_call(place, own, rest, mine, other, width):
    inner = BOUNDS[4]
    rows = own.shape[0] - 2 * inner
    return pl.pallas_call(
        unpack_body,
        in_specs=[pl.BlockSpec(memory_space=pltpu.SMEM)]
        + [pl.BlockSpec(memory_space=pltpu.VMEM)] * 4,
        out_shape=[
            shaped((inner, width), BF16),
            shaped((inner, width), BF16),
            shaped((rows, width), F32),
            shaped((rows, width), F32),
        ],
        name="unpack_small",
    )(place, own, rest, mine, other)


def small_call(body, name, shape, dtype, core, *arrays):
    return pl.pallas_call(
        body,
        in_specs=[pl.BlockSpec(memory_space=pltpu.SMEM)]
        + [pl.BlockSpec(memory_space=pltpu.VMEM)] * len(arrays),
        out_shape=shaped(shape, dtype),
        name=name,
    )(core, *arrays)


def hop_call(body, name, old, add, through):
    return pl.pallas_call(body, out_shape=shaped(add.shape, BF16), name=name)(old, add, through)


def gather_three_call(one, two, three):
    return pl.pallas_call(
        gather_three_body, out_shape=shaped(three.shape, BF16), name="state_gather"
    )(one, two, three)


def gather_back_call(one, two, three, t_one, t_two):
    return pl.pallas_call(
        gather_back_body, out_shape=shaped(three.shape, BF16), name="state_gather_back"
    )(one, two, three, t_one, t_two)


def matmul(left, right):
    return jnp.dot(left, right, preferred_element_type=F32)


def matmul_nt(left, right):
    return lax.dot_general(left, right, NT, preferred_element_type=F32)


def matmul_tn(left, right):
    return lax.dot_general(left, right, TN, preferred_element_type=F32)


def layer_norm(values, gain, bias_row):
    center = values - jnp.mean(values, axis=-1, keepdims=True)
    spread_sq = jnp.mean(center * center, axis=-1, keepdims=True)
    return center * lax.rsqrt(spread_sq + LN_EPS) * gain + bias_row


def blend_rows(current, earlier, keep_row, gain_rows):
    change = earlier * keep_row - current
    return current[None] + change[None] * gain_rows[:, None, :]


def shifted(value, steps):
    count = lax.axis_size("seq")
    initial, last = (max(0, -steps), min(count, count - steps))
    return lax.ppermute(value, "seq", [(place, place + steps) for place in range(initial, last)])


def partner(value, axis, flip):
    count = lax.axis_size(axis)
    return lax.ppermute(value, axis, [(place, place ^ flip) for place in range(count)])


def after(value, *others):
    return lax.optimization_barrier((value,) + others)[0]


def spread_to_group(shard):
    count = lax.axis_size("fsdp")
    return [shard] + [partner(shard, "fsdp", flip) for flip in range(1, count)]


def relay_to_group(shard, axis):
    if lax.axis_size("fsdp") != 4:
        return spread_to_group(shard)
    first = partner(shard, "fsdp", 1)
    second = partner(shard, "fsdp", 2)
    size = shard.shape[axis] // 2
    low = partner(lax.slice_in_dim(first, 0, size, axis=axis), "fsdp", 2)
    high = partner(lax.slice_in_dim(second, size, 2 * size, axis=axis), "fsdp", 1)
    return [shard, first, second, jnp.concatenate([low, high], axis=axis)]


def absolute_order(pieces, me, axis):
    stack = jnp.stack(pieces)
    ordered = [
        lax.dynamic_index_in_dim(stack, me ^ place, 0, False) for place in range(len(pieces))
    ]
    return jnp.concatenate(ordered, axis=axis)


def relative_columns(array, me, count):
    size = array.shape[1] // count
    pieces = [
        lax.dynamic_slice_in_dim(array, (me ^ place) * size, size, 1) for place in range(count)
    ]
    return jnp.concatenate(pieces, axis=1)


def core_halves(array, axis, core):
    size = array.shape[axis] // 2
    mine = lax.dynamic_slice_in_dim(array, core * size, size, axis)
    return (mine, lax.dynamic_slice_in_dim(array, (1 - core) * size, size, axis))


def by_core(core, mine, other):
    return (jnp.where(core == 0, mine, other), jnp.where(core == 0, other, mine))


def join_halves(core, mine, other, axis):
    return jnp.concatenate(by_core(core, mine, other), axis=axis)


def gather_rows(rows):
    return jnp.concatenate(spread_to_group(rows), axis=0)


def scatter_rows(rows):
    count = lax.axis_size("fsdp")
    size = rows.shape[0] // count
    total = rows[:size].astype(F32)
    for flip in range(1, count):
        total = total + partner(rows[flip * size : (flip + 1) * size], "fsdp", flip).astype(F32)
    return total


def column_pieces(array, count):
    size = array.shape[-1] // count
    return [array[..., place * size : (place + 1) * size] for place in range(count)]


def exchange(pieces):
    return [pieces[0]] + [
        partner(pieces[flip], "fsdp", flip) for flip in range(1, len(pieces))
    ]


def as_blocks(pieces):
    if pieces[0].shape[-1] == BLOCK:
        return jnp.stack(pieces)
    joined = jnp.concatenate(pieces, axis=-1)
    split = joined.reshape(joined.shape[:-1] + (-1, BLOCK))
    return jnp.moveaxis(split, -2, 0)


def from_blocks(blocks, count):
    if blocks.shape[0] == count:
        return [blocks[place] for place in range(count)]
    joined = jnp.moveaxis(blocks, 0, -2)
    joined = joined.reshape(joined.shape[:-2] + (-1,))
    return column_pieces(joined, count)


def sum_on_chip(array, core):
    chips = lax.axis_size("seq") // 2
    own, leaving = core_halves(array, 0, core)
    other = partner(leaving, "seq", 1)
    summed = (own.astype(F32) + other.astype(F32)).astype(BF16)
    return summed.reshape(chips, array.shape[0] // (2 * chips), -1)


def sum_over_chips(on_chip, chip):
    total = lax.dynamic_index_in_dim(on_chip, chip, 0, False).astype(F32)
    for flip in range(1, on_chip.shape[0]):
        leaving = lax.dynamic_index_in_dim(on_chip, chip ^ flip, 0, False)
        total = total + partner(leaving, "seq", 2 * flip).astype(F32)
    return total.astype(BF16)


def share_sums(total, core, chip):
    chips = lax.axis_size("seq") // 2
    pieces = [total[None]]
    for flip in range(1, chips):
        pieces.append(partner(total, "seq", 2 * flip)[None])
    mine = absolute_order(pieces, chip, 0)
    return by_core(core, mine, partner(mine, "seq", 1))


def own_pairs(core, array):
    size = array.shape[0] // 2
    return lax.dynamic_slice_in_dim(array, core * size, size, 0)


def all_pairs(core, mine):
    return join_halves(core, mine, partner(mine, "seq", 1), 0)


def body(
    layer_input,
    first_layer_values,
    document_numbers,
    output_cotangent,
    projection_matrices,
    time_output_matrix,
    lowrank_first,
    lowrank_second,
    channel_key_matrix,
    channel_value_matrix,
    vectors,
):
    groups = lax.axis_size("fsdp")
    me = lax.axis_index("fsdp")
    place = lax.axis_index("seq")
    core = place % 2
    chip = place // 2
    chips = lax.axis_size("seq") // 2
    span, width = layer_input.shape[1:]
    here = projection_matrices.shape[2]
    resid_in = layer_input[0].astype(F32)
    cotangent = output_cotangent[0]
    id_plus = document_numbers[0].astype(F32) + 1.0

    edge = jnp.concatenate(
        [resid_in[span - 1 :], jnp.broadcast_to(id_plus[span - 1 :, None], (1, PAIR))], axis=1
    )
    edge = shifted(edge, 1)
    core_flag = core.reshape(1)
    inner = BOUNDS[4]
    vec_count = vectors.shape[0]
    packed = jnp.concatenate(
        [
            lowrank_first.T,
            lowrank_second,
            jnp.concatenate([vectors, jnp.zeros((32 - vec_count, here), BF16)], axis=0),
        ],
        axis=0,
    )
    if here == BLOCK:
        pack_own, pack_rest = core_halves(packed, 1, core)
        pack_mine = jnp.stack(spread_to_group(pack_own)[1:])
        pack_other = partner(pack_mine, "seq", 1)
        down, second, vec_rows, vec = unpack_call(
            jnp.stack([core, me]), pack_own, pack_rest, pack_mine, pack_other, width
        )
    else:
        pack_pieces = spread_to_group(packed)
        relative = jnp.concatenate(pack_pieces, axis=1)
        ordered_pack = absolute_order(pack_pieces, me, 1)
        down = ordered_pack[:inner]
        second = relative[inner : 2 * inner]
        vec_rows = relative[2 * inner :].astype(F32)
        vec = ordered_pack[2 * inner :].astype(F32)
    own_proj, rest_proj = core_halves(projection_matrices, 1, core)
    proj_mine = relay_to_group(own_proj, 1)
    first_rel = relative_columns(first_layer_values[0], me, groups)

    edge_id = edge[0, width]
    earlier_ids = jnp.concatenate([edge[0, width : width + 1], id_plus[:-1]])
    keep_row = (id_plus == earlier_ids).astype(F32)[:, None]
    segment = id_plus - edge_id
    seg_col = jnp.broadcast_to(segment[:, None], (span, PAIR))
    seg_row = jnp.broadcast_to(segment[None], (8, span))

    def mixer(current, earlier, gain_rows):
        return blend_rows(current, earlier, keep_row, gain_rows)

    normed_one, ln_one_back = jax.vjp(layer_norm, resid_in, vec[14], vec[15])
    edge_row = layer_norm(edge[:, :width], vec[14], vec[15])
    earlier_one = jnp.concatenate([edge_row, normed_one[:-1]])
    mixed_rows, mix_back = jax.vjp(mixer, normed_one, earlier_one, vec[0:6])
    mixed = mixed_rows.astype(BF16)
    down_parts = [down[BOUNDS[part] : BOUNDS[part + 1]] for part in range(4)]
    decay_pre = matmul_nt(mixed[1], down_parts[0])
    low_decay = jnp.tanh(decay_pre).astype(BF16)
    low_alpha = matmul_nt(mixed[4], down_parts[1]).astype(BF16)
    low_vmix = matmul_nt(mixed[3], down_parts[2]).astype(BF16)
    gate_pre = matmul_nt(mixed[5], down_parts[3])
    low_gate = jax.nn.sigmoid(gate_pre).astype(BF16)
    lows = (low_decay, low_alpha, low_vmix, low_gate)
    mix_three = jnp.stack([mixed[0], mixed[2], mixed[3]])
    mix_halves = core_halves(mix_three, 2, core)

    if here == BLOCK:
        pieces = proj_mine
    else:
        pieces = [jnp.concatenate(proj_mine, axis=2)]
        rest_proj = partner(pieces[0], "seq", 1)
    chunk = width // len(pieces)
    results = None
    weights = []
    for base, piece in enumerate(pieces):
        lanes = slice(base * chunk, (base + 1) * chunk)
        if base == 0:
            pair = (piece, rest_proj)
        else:
            pair = (piece, partner(piece, "seq", 1))
        weights.append(pair)
        results = forward_call(
            mix_halves, pair, lows, second[:, lanes], first_rel[:, lanes],
            vec_rows[:, lanes], seg_col, seg_row, base, width, results,
        )
        if here == BLOCK and base == 2:
            pieces[3] = after(pieces[3], results[-1])
    raws = results[0:6]
    gate, query, y_part, u_part, out_part, bonus, inverse, both = results[6:]

    out_pieces = spread_to_group(after(core_halves(time_output_matrix, 0, core)[0], both))
    cot_rows = gather_rows(after(cotangent, both))
    mix_pieces = spread_to_group(after(mix_three, both))

    other_both = partner(both, "seq", 1)
    pairs = both.shape[1]
    own = pairs // 2
    chip_both = small_call(
        merge_body, "state_merge", (2 * own,) + both.shape[2:], BF16, core_flag, both, other_both
    )
    chip_offset = chip_both[:own]
    chip_transfer = chip_both[own:]
    if chips == 4:
        arriving = gather_three_call(
            shifted(chip_both, 2), shifted(chip_both, 4), shifted(chip_offset, 6)
        )
        next_transfers = (shifted(chip_transfer, -2), shifted(chip_transfer, -4))
    else:
        arriving = shifted(chip_offset, 2)
        for _ in range(chips - 2):
            arriving = shifted(
                hop_call(hop_body, "state_hop", arriving, chip_offset, chip_transfer), 2
            )
    out_pieces = lax.optimization_barrier(tuple(out_pieces) + (arriving,))[:-1]
    out_mine = jnp.stack(out_pieces)
    out_full = join_halves(core, out_mine, partner(out_mine, "seq", 1), 1).reshape(width, width)
    state = small_call(
        state_body, "state_final", both.shape[1:], F32,
        core_flag, arriving, partner(arriving, "seq", 1), other_both,
    )

    xhat, rstd, branch = finish_call(query, out_part, bonus, state, gate, vec_rows)
    middle = resid_in + matmul(branch, out_full)
    normed_two, ln_two_back = jax.vjp(layer_norm, middle, vec[16], vec[17])
    edge_two = shifted(normed_two[span - 1 :], 1)
    earlier_two = jnp.concatenate([edge_two, normed_two[:-1]])
    cmix_in, cmix_back = jax.vjp(mixer, normed_two, earlier_two, vec[18:19])
    cmix_rows = gather_rows(cmix_in[0].astype(BF16))
    pre_act = matmul(cmix_rows, channel_key_matrix)
    d_hidden = matmul_nt(cot_rows, channel_value_matrix)
    active = jax.nn.relu(pre_act)
    d_pre = (d_hidden * 2.0 * active).astype(BF16)
    d_cmix = scatter_rows(matmul_nt(d_pre, channel_key_matrix).astype(BF16))
    hidden = jnp.square(active).astype(BF16)
    grad_value = matmul_tn(hidden, cot_rows).astype(BF16)
    grad_key = matmul_tn(cmix_rows, d_pre).astype(BF16)
    hidden_out = matmul(hidden, channel_value_matrix).astype(BF16)
    d_cmix, grad_value, grad_key, hidden_out = lax.optimization_barrier(
        (d_cmix, grad_value, grad_key, hidden_out)
    )
    hidden_parts = [hidden_out[at * span : (at + 1) * span] for at in range(groups)]
    grad_value, grad_key = [
        part.astype(F32) for part in lax.psum((grad_value, grad_key), "seq")
    ]

    d_normed_two, d_earlier_two, d_cmix_gain = cmix_back(d_cmix[None])
    back_two = shifted(d_earlier_two[:1], -1)
    d_middle, d_gain_two, d_bias_two = ln_two_back(
        d_normed_two + jnp.concatenate([d_earlier_two[1:], back_two])
    )
    d_middle = d_middle + cotangent.astype(F32)
    d_middle_b = d_middle.astype(BF16)
    d_branch = matmul_nt(d_middle_b, out_full)
    d_out, d_inner, d_gate, start_grad, vec_early = early_call(
        d_branch, gate, xhat, rstd, bonus, query, vec_rows
    )

    other_start = partner(start_grad, "seq", 1)
    chip_start = small_call(
        merge_back_body, "grad_merge", (own,) + start_grad.shape[1:], BF16,
        core_flag, start_grad, other_start, both, other_both,
    )
    if chips == 4:
        arriving = gather_back_call(
            shifted(chip_start, -2), shifted(chip_start, -4), shifted(chip_start, -6),
            *next_transfers,
        )
    else:
        arriving = shifted(chip_start, -2)
        for _ in range(chips - 2):
            arriving = shifted(
                hop_call(hop_back_body, "grad_hop", arriving, chip_start, chip_transfer), -2
            )
    end_grad = small_call(
        end_body, "grad_final", both.shape[1:], F32,
        core_flag, arriving, partner(arriving, "seq", 1), other_start, other_both,
    )

    three, d_first_rel, ups, mixed_mine, mixed_other, *d_lows = late_call(
        raws, first_rel, vec_rows, seg_col, seg_row,
        inverse, y_part, u_part, state, end_grad, d_out, d_inner, d_gate,
        vec_early, second, lows, weights,
    )

    middle_pieces = spread_to_group(d_middle_b)
    held = lax.optimization_barrier(tuple(mix_pieces) + tuple(middle_pieces) + (three,))
    mix_rows = jnp.concatenate(held[:groups], axis=1)
    middle_rows = jnp.concatenate(held[groups : 2 * groups], axis=0)
    three = held[-1]
    branch_cols = jnp.concatenate(exchange(column_pieces(branch, groups)), axis=0)
    grad_out = matmul_tn(branch_cols, middle_rows)
    grad_out = jnp.concatenate(column_pieces(grad_out, width // here), axis=0)
    head_grads = jnp.concatenate(exchange(from_blocks(three, groups)), axis=1)
    grad_proj = [matmul_tn(mix_rows[part], head_grads[part]) for part in range(3)]
    large = jnp.concatenate(grad_proj + [grad_out], axis=0).astype(BF16)
    large = sum_on_chip(large, core)
    mixed_mine, mixed_other, large = lax.optimization_barrier((mixed_mine, mixed_other, large))
    hidden_pieces = exchange(lax.optimization_barrier(tuple(hidden_parts) + (large,))[:-1])
    large = sum_over_chips(large, chip)
    tanh_now = jnp.tanh(decay_pre)
    sigma_now = jax.nn.sigmoid(gate_pre)
    low_grads = (
        (d_lows[0] * (1.0 - tanh_now * tanh_now)).astype(BF16),
        d_lows[1].astype(BF16),
        d_lows[2].astype(BF16),
        (d_lows[3] * sigma_now * (1.0 - sigma_now)).astype(BF16),
    )
    low_mixes = (mixed[1], mixed[4], mixed[3], mixed[5])
    grad_down = jnp.concatenate(
        [matmul_tn(low_grads[part], low_mixes[part]) for part in range(4)], axis=0
    )
    d_wide = join_halves(core, mixed_mine, mixed_other, 2)
    d_mixed = jnp.stack(
        [
            d_wide[0],
            matmul(low_grads[0], down_parts[0]),
            d_wide[1],
            d_wide[2] + matmul(low_grads[2], down_parts[2]),
            matmul(low_grads[1], down_parts[1]),
            matmul(low_grads[3], down_parts[3]),
        ]
    )
    d_normed_one, d_earlier_one, d_mix_gains = mix_back(d_mixed)
    back_one = shifted(d_earlier_one[:1], -1)
    d_resid, d_gain_one, d_bias_one = ln_one_back(
        d_normed_one + jnp.concatenate([d_earlier_one[1:], back_one])
    )
    d_input = d_resid + d_middle

    rows_here = lax.broadcasted_iota(jnp.int32, (16, 1), 0)
    vec_part = jnp.pad(d_mix_gains, ((0, 10), (0, 0)))
    singles = (d_gain_one, d_bias_one, d_gain_two, d_bias_two, d_cmix_gain[0])
    for at, row in enumerate(singles):
        vec_part = vec_part + jnp.where(rows_here == 6 + at, row[None], 0.0)
    ordered = jnp.concatenate([grad_down.astype(BF16), vec_part.astype(BF16)], axis=0)
    up_pieces = from_blocks(ups, groups)
    fill = -2 * (inner + 16) % (32 * chips)
    small = [
        jnp.concatenate(
            [
                up_pieces[at],
                lax.dynamic_slice_in_dim(ordered, (me ^ at) * here, here, 1),
                jnp.zeros((fill, here), BF16),
            ],
            axis=0,
        )
        for at in range(groups)
    ]
    landed = exchange(small)
    total = landed[0].astype(F32)
    for piece in landed[1:]:
        total = total + piece.astype(F32)
    block_out = middle
    for piece in hidden_pieces:
        block_out = block_out + piece.astype(F32)
    total, large, grad_key, grad_value, block_out = lax.optimization_barrier(
        (total.astype(BF16), large, grad_key, grad_value, block_out.astype(BF16))
    )
    total = sum_over_chips(sum_on_chip(total, core), chip)
    part = large.shape[0]
    low, high = share_sums(jnp.concatenate([large, total], axis=0), core, chip)
    large_low, large_high = [side[:, :part].reshape(-1, here) for side in (low, high)]
    total = jnp.concatenate(
        [side[:, part:].reshape(-1, here) for side in (low, high)], axis=0
    ).astype(F32)
    down_at = inner + 16
    mix_at = down_at + inner
    grad_vec = jnp.concatenate(
        [
            total[mix_at : mix_at + 6],
            total[inner : inner + 6],
            total[inner + 8 : inner + 10],
            total[mix_at + 6 : mix_at + 11],
        ],
        axis=0,
    )
    return (
        block_out[None],
        d_input[None],
        relative_columns(d_first_rel, me, groups)[None],
        jnp.stack([large_low[:width], large_low[width:], large_high[:width]]).astype(F32),
        jnp.concatenate(
            [large_high[width + at : width + at + here] for at in range(0, width, here)], axis=1
        ).astype(F32),
        total[down_at:mix_at].T,
        total[:inner],
        grad_key,
        grad_value,
        grad_vec,
    )


def solution(mesh):
    in_specs = (
        P("fsdp", "seq", None),
        P("fsdp", "seq", None),
        P("fsdp", "seq"),
        P("fsdp", "seq", None),
        P(None, None, "fsdp"),
        P("fsdp", None),
        P("fsdp", None),
        P(None, "fsdp"),
        P(None, "fsdp"),
        P("fsdp", None),
        P(None, "fsdp"),
    )
    out_specs = (
        P("fsdp", "seq", None),
        P("fsdp", "seq", None),
        P("fsdp", "seq", None),
        P(None, None, "fsdp"),
        P("fsdp", None),
        P("fsdp", None),
        P(None, "fsdp"),
        P(None, "fsdp"),
        P("fsdp", None),
        P(None, "fsdp"),
    )
    return jax.shard_map(body, mesh=mesh, in_specs=in_specs, out_specs=out_specs, check_vma=False)
```
